32 devices in a mesh: dp: 8 (over y, x, core), tensor: 4 (over z).
Axes of the slice: x: 2, y: 2, z: 4, core: 2. Of those that a mesh axis runs over, the one named last changes fastest.
Arguments:
- hidden_in: bfloat16 [16384, 1024], P('dp'), may hold values from -6 to 6
- lengths: int32 [8], P('dp'), may hold values from 512 to 2048, as said below
- query_weight: bfloat16 [1024, 1024], P(None, 'tensor'), may hold values from -0.1875 to 0.1875
- query_bias: bfloat16 [1024], P('tensor'), may hold values from -1 to 1
- key_weight: bfloat16 [1024, 1024], P(None, 'tensor'), may hold values from -0.1875 to 0.1875
- value_weight: bfloat16 [1024, 1024], P(None, 'tensor'), may hold values from -0.1875 to 0.1875
- value_bias: bfloat16 [1024], P('tensor'), may hold values from -1 to 1
- output_weight: bfloat16 [1024, 1024], P(None, 'tensor'), may hold values from -2 to 2
- output_bias: bfloat16 [1024], replicated, may hold values from -1 to 1
- first_gain: bfloat16 [1024], replicated, may hold values from 0.5 to 1.5
- first_shift: bfloat16 [1024], replicated, may hold values from -1 to 1
- inner_weight: bfloat16 [1024, 4096], P(None, 'tensor'), may hold values from -0.1875 to 0.1875
- inner_bias: bfloat16 [4096], P('tensor'), may hold values from -1 to 1
- outer_weight: bfloat16 [1024, 4096], P(None, 'tensor'), may hold values from -0.125 to 0.125
- outer_bias: bfloat16 [1024], replicated, may hold values from -1 to 1
- second_gain: bfloat16 [1024], replicated, may hold values from 0.5 to 1.5
- second_shift: bfloat16 [1024], replicated, may hold values from -1 to 1
- cotangent: bfloat16 [16384, 1024], P('dp'), may hold values from -6 to 6
- teacher: bfloat16 [16384, 1024], P('dp'), may hold values from -6 to 6
Outputs:
- layer_output: bfloat16 [16384, 1024], P(('dp', 'tensor'))
- distill_loss: float32 [], replicated
- input_grad: float32 [16384, 1024], P(('dp', 'tensor'))
- query_weight_grad: float32 [1024, 1024], P('dp', 'tensor')
- query_bias_grad: float32 [1024], replicated
- key_weight_grad: float32 [1024, 1024], P('dp', 'tensor')
- value_weight_grad: float32 [1024, 1024], P('dp', 'tensor')
- value_bias_grad: float32 [1024], replicated
- output_weight_grad: float32 [1024, 1024], P('dp', 'tensor')
- output_bias_grad: float32 [1024], replicated
- first_gain_grad: float32 [1024], replicated
- first_shift_grad: float32 [1024], replicated
- inner_weight_grad: float32 [1024, 4096], P('dp', 'tensor')
- inner_bias_grad: float32 [4096], replicated
- outer_weight_grad: float32 [1024, 4096], P('dp', 'tensor')
- outer_bias_grad: float32 [1024], replicated
- second_gain_grad: float32 [1024], replicated
- second_shift_grad: float32 [1024], replicated
The draws below stay inside these ranges and needn't reach their ends.
Inputs may be any that keep to these rules, and one draw needn't show every extreme that they name: `lengths`: one sequence's valid tokens; slots after them are padding; some sequence fills all 2048 slots.
All inputs are finite; a program needn't handle non-finite values.
Results may differ from the reference program's by a relative error of at most 0.018.
Values may be sent and summed in bfloat16 or wider, within the bound.
No kernel may reach another device: no remote copies, remote signals or barrier semaphores. Data moves between devices by JAX's collectives and lax.ppermute only.
A program may use at most 256 MiB of HBM per device.

```python
import math
import jax
import jax.numpy as jnp
from jax import lax

D = 1024
H = 16
HD = 64
FF = 4096
LEN = 2048
SEQS = 8
TOKENS = 16384


def draw_lengths(key, part):
    seq_index = jnp.arange(SEQS, dtype=jnp.int32)
    baseline = LEN // 3 + (LEN - LEN // 3) * seq_index // max(SEQS - 1, 1)
    jitter = jax.random.randint(key, (SEQS,), -(LEN // 16), LEN // 16 + 1, dtype=jnp.int32)
    lengths_drawn = jnp.clip(baseline + jitter, 1, LEN)
    return jnp.where(seq_index == SEQS - 1, LEN, lengths_drawn).astype(jnp.int32)


def levels(stream_key, shape, split, low, largest):
    def one(dim, parts):
        heights = jax.random.uniform(jax.random.fold_in(jax.random.fold_in(stream_key, 6), dim), (parts,), jnp.float32, low / len(split), largest / len(split))
        return jnp.repeat(jnp.exp(heights), shape[dim] // parts).reshape((-1,) + (1,) * (len(shape) - dim - 1))

    level = one(*split[0])
    for cut in split[1:]:
        level = level * one(*cut)
    return level


def noise(rng, extent, deviation, bound, split=(), kind=jnp.bfloat16):
    factor_of = levels(rng, extent, split, -0.22, 0.18) if split else 1.0
    entries = jax.random.normal(rng, extent, jnp.float32) * deviation * factor_of
    return jnp.minimum(jnp.maximum(entries, -bound), bound).astype(kind)


def setup_inputs(seed: int = 0) -> dict:
    key_list = jax.random.split(jax.random.key(seed), 20)
    hidden_in = noise(key_list[0], (TOKENS, D), 1.0, 6.0, ((0, 8),))
    lengths = draw_lengths(jax.random.fold_in(key_list[19], 71), 0)
    query_weight = noise(key_list[2], (D, D), D ** -0.5, 0.1875, ((1, 4),))
    query_bias = noise(key_list[3], (D,), 0.2, 1.0, ((0, 4),))
    key_weight = noise(key_list[4], (D, D), D ** -0.5, 0.1875, ((1, 4),))
    value_weight = noise(key_list[5], (D, D), D ** -0.5, 0.1875, ((1, 4),))
    value_bias = noise(key_list[6], (D,), 0.2, 1.0, ((0, 4),))
    output_weight = noise(key_list[7], (D, D), 8 ** -0.5, 2.0, ((1, 4),))
    output_bias = noise(key_list[8], (D,), 0.2, 1.0)
    first_gain = jnp.clip(1.0 + 0.1 * jax.random.normal(key_list[9], (D,), jnp.float32), 0.5, 1.5).astype(jnp.bfloat16)
    first_shift = noise(key_list[10], (D,), 0.2, 1.0)
    inner_weight = noise(key_list[11], (D, FF), D ** -0.5, 0.1875, ((1, 4),))
    inner_bias = noise(key_list[12], (FF,), 0.2, 1.0, ((0, 4),))
    outer_weight = noise(key_list[13], (D, FF), (FF // 2) ** -0.5, 0.125, ((1, 4),))
    outer_bias = noise(key_list[14], (D,), 0.2, 1.0)
    second_gain = jnp.clip(1.0 + 0.1 * jax.random.normal(key_list[15], (D,), jnp.float32), 0.5, 1.5).astype(jnp.bfloat16)
    second_shift = noise(key_list[16], (D,), 0.2, 1.0)
    cotangent = noise(key_list[17], (TOKENS, D), 1.0, 6.0, ((0, 8),))
    teacher = noise(key_list[18], (TOKENS, D), 1.0, 6.0, ((0, 8),))
    return {"hidden_in": hidden_in, "lengths": lengths, "query_weight": query_weight, "query_bias": query_bias, "key_weight": key_weight, "value_weight": value_weight, "value_bias": value_bias, "output_weight": output_weight, "output_bias": output_bias, "first_gain": first_gain, "first_shift": first_shift, "inner_weight": inner_weight, "inner_bias": inner_bias, "outer_weight": outer_weight, "outer_bias": outer_bias, "second_gain": second_gain, "second_shift": second_shift, "cotangent": cotangent, "teacher": teacher}


@jax.custom_vjp
def low(v):
    return lax.optimization_barrier(v.astype(jnp.bfloat16)).astype(jnp.float32)

@jax.custom_vjp
def low_back(v):
    return v

def low_keep(v):
    return (low(v), None)

def low_pass(kept, grad):
    return (grad,)

def back_keep(v):
    return (v, None)

def back_low(kept, grad):
    return (low(grad),)
low.defvjp(low_keep, low_pass)
low_back.defvjp(back_keep, back_low)
epsilon = 1e-05

def matmul(former, latter):
    return jnp.dot(former, latter, precision=lax.Precision.HIGHEST)

def layer_norm(hidden, norm_gain, norm_shift):
    centered = hidden - lax.optimization_barrier(jnp.mean(hidden, axis=-1, keepdims=True))
    inverse = lax.rsqrt(lax.optimization_barrier(jnp.mean(centered * centered, axis=-1, keepdims=True)) + epsilon)
    return centered * inverse * norm_gain + norm_shift

def gelu_exact(values):
    return 0.5 * values * (1.0 + jax.scipy.special.erf(values * 0.7071067811865476))

def one_sequence(weights, hidden, length_here):
    query_weight, query_bias, key_weight, value_weight, value_bias, output_weight, output_bias, first_gain, first_shift, inner_weight, inner_bias, outer_weight, outer_bias, second_gain, second_shift = weights
    score_scale = 1.0 / math.sqrt(HD)
    queries = low_back(low(matmul(hidden, query_weight) + query_bias)).reshape(LEN, H, HD)
    keys_all = low_back(low(matmul(hidden, key_weight))).reshape(LEN, H, HD)
    values_all = low_back(low(matmul(hidden, value_weight) + value_bias)).reshape(LEN, H, HD)
    scores = jnp.einsum('qhd,khd->hqk', queries, keys_all, precision=lax.Precision.HIGHEST) * score_scale
    key_valid = jnp.arange(LEN) < length_here
    scores = low_back(jnp.where(key_valid[None, None, :], scores, -1e+30))
    row_peak = lax.optimization_barrier(jnp.max(scores, axis=-1, keepdims=True))
    exponent = jnp.exp(scores - row_peak)
    probs = exponent / lax.optimization_barrier(jnp.sum(exponent, axis=-1, keepdims=True))
    context = jnp.einsum('hqk,khd->qhd', low(probs), values_all, precision=lax.Precision.HIGHEST)
    context = low_back(low(context.reshape(LEN, D)))
    attention = low_back(matmul(context, output_weight.T) + output_bias)
    normed = layer_norm(hidden + attention, first_gain, first_shift)
    inner = low_back(matmul(low(normed), inner_weight) + inner_bias)
    branch = low_back(matmul(low(gelu_exact(inner)), outer_weight.T) + outer_bias)
    return layer_norm(normed + branch, second_gain, second_shift)

def reference(hidden_in, lengths, query_weight, query_bias, key_weight, value_weight, value_bias, output_weight, output_bias, first_gain, first_shift, inner_weight, inner_bias, outer_weight, outer_bias, second_gain, second_shift, cotangent, teacher):
    weights = tuple((array_in.astype(jnp.float32) for array_in in (query_weight, query_bias, key_weight, value_weight, value_bias, output_weight, output_bias, first_gain, first_shift, inner_weight, inner_bias, outer_weight, outer_bias, second_gain, second_shift)))
    hidden_all = hidden_in.astype(jnp.float32).reshape(SEQS, LEN, D)
    upstream_all = cotangent.astype(jnp.float32).reshape(SEQS, LEN, D)
    teacher_all = teacher.astype(jnp.float32).reshape(SEQS, LEN, D)
    token_total = jnp.sum(lengths).astype(jnp.float32)
    checked_sequence = jax.checkpoint(one_sequence)

    def objective(weights, hidden_all):

        def step_one(carry, inputs):
            hidden_seq, length_here, upstream_seq, teacher_seq = inputs
            final = checked_sequence(weights, hidden_seq, length_here)
            row_mask = (jnp.arange(LEN) < length_here).astype(jnp.float32)[:, None]
            linear = jnp.sum(row_mask * upstream_seq * final)
            error = final - teacher_seq
            squared = jnp.sum(row_mask * error * error)
            return ((carry[0] + linear, carry[1] + squared), final)
        zero_value = jnp.zeros((), jnp.float32)
        (linear, squared), finals = lax.scan(step_one, (zero_value, zero_value), (hidden_all, lengths, upstream_all, teacher_all))
        loss_value = squared / token_total
        return (linear + TOKENS / 4.0 * loss_value, (finals, loss_value))
    total_value, pullback, (finals, loss_value) = jax.vjp(objective, weights, hidden_all, has_aux=True)
    weight_grads, hidden_grad = pullback(jnp.ones((), jnp.float32))
    query_weight_grad, query_bias_grad, key_weight_grad, value_weight_grad, value_bias_grad, output_weight_grad, output_bias_grad, first_gain_grad, first_shift_grad, inner_weight_grad, inner_bias_grad, outer_weight_grad, outer_bias_grad, second_gain_grad, second_shift_grad = weight_grads
    return (finals.reshape(TOKENS, D).astype(jnp.bfloat16), loss_value, hidden_grad.reshape(TOKENS, D), query_weight_grad, query_bias_grad, key_weight_grad, value_weight_grad, value_bias_grad, output_weight_grad, output_bias_grad, first_gain_grad, first_shift_grad, inner_weight_grad, inner_bias_grad, outer_weight_grad, outer_bias_grad, second_gain_grad, second_shift_grad)
```

```python
import math

import jax
import jax.numpy as jnp
from jax import lax
from jax.sharding import PartitionSpec as P

HD = 64


epsilon = 1e-05


def matmul(former, latter):
    return jnp.dot(former, latter, preferred_element_type=jnp.float32)


def times_rows(former, latter):
    return lax.dot_general(
        former, latter, (((1,), (1,)), ((), ())), preferred_element_type=jnp.float32
    )


def over_rows(former, latter):
    return lax.dot_general(
        former, latter, (((0,), (0,)), ((), ())), preferred_element_type=jnp.float32
    )


def layer_norm(hidden, norm_gain, norm_shift):
    centered = hidden - jnp.mean(hidden, axis=-1, keepdims=True)
    inverse = lax.rsqrt(jnp.mean(centered * centered, axis=-1, keepdims=True) + epsilon)
    normal = centered * inverse
    return (normal * norm_gain + norm_shift, normal, inverse)


def norm_back(upstream, normal, inverse, norm_gain):
    scaled = upstream * norm_gain
    return inverse * (
        scaled
        - jnp.mean(scaled, axis=-1, keepdims=True)
        - normal * jnp.mean(scaled * normal, axis=-1, keepdims=True)
    )


def gelu_parts(values):
    cumulative = 0.5 * (1.0 + jax.scipy.special.erf(values * 0.7071067811865476))
    slope = cumulative + values * jnp.exp(-0.5 * values * values) * 0.3989422804014327
    return (values * cumulative, slope)


def split_blocks(queries, keys_all, values_all):
    seq_len, local_width = queries.shape
    heads_here = local_width // HD
    block_rows = min(512, seq_len)
    block_count = seq_len // block_rows
    keys_split = keys_all.reshape(seq_len, heads_here, HD)
    values_split = values_all.reshape(seq_len, heads_here, HD)
    query_blocks = queries.reshape(block_count, block_rows, heads_here, HD)
    return (keys_split, values_split, query_blocks, block_count, block_rows, heads_here)


def block_scores(query_block, keys_split, key_valid, score_scale):
    scores = (
        jnp.einsum("qhd,khd->hqk", query_block, keys_split, preferred_element_type=jnp.float32)
        * score_scale
    )
    return jnp.where(key_valid[None, None, :], scores, -1e30)


def attend_forward(queries, keys_all, values_all, key_valid, score_scale):
    keys_split, values_split, query_blocks, block_count, block_rows, heads_here = split_blocks(
        queries, keys_all, values_all
    )

    def one_block(query_block):
        scores = block_scores(query_block, keys_split, key_valid, score_scale)
        row_peak = jnp.max(scores, axis=-1, keepdims=True)
        exponent = jnp.exp(scores - row_peak)
        row_total = jnp.sum(exponent, axis=-1, keepdims=True)
        probs = (exponent / row_total).astype(jnp.bfloat16)
        context = jnp.einsum(
            "hqk,khd->qhd", probs, values_split, preferred_element_type=jnp.float32
        )
        return (context, (row_peak + jnp.log(row_total))[..., 0])

    context, logsum = lax.map(one_block, query_blocks)
    return (context.reshape(queries.shape), logsum)


def attend_backward(queries, keys_all, values_all, key_valid, score_scale, logsum, context_grad):
    keys_split, values_split, query_blocks, block_count, block_rows, heads_here = split_blocks(
        queries, keys_all, values_all
    )
    grad_blocks = context_grad.reshape(block_count, block_rows, heads_here, HD)

    def one_block(carry, inputs):
        key_sum, value_sum = carry
        query_block, grad_block, logsum_block = inputs
        scores = block_scores(query_block, keys_split, key_valid, score_scale)
        probs = jnp.exp(scores - logsum_block[..., None])
        prob_grad = jnp.einsum(
            "qhd,khd->hqk", grad_block, values_split, preferred_element_type=jnp.float32
        )
        centre = jnp.sum(probs * prob_grad, axis=-1, keepdims=True)
        score_grad = (probs * (prob_grad - centre)).astype(jnp.bfloat16)
        query_grad = (
            jnp.einsum("hqk,khd->qhd", score_grad, keys_split, preferred_element_type=jnp.float32)
            * score_scale
        )
        key_sum = (
            key_sum
            + jnp.einsum(
                "hqk,qhd->khd", score_grad, query_block, preferred_element_type=jnp.float32
            )
            * score_scale
        )
        value_sum = value_sum + jnp.einsum(
            "hqk,qhd->khd",
            probs.astype(jnp.bfloat16),
            grad_block,
            preferred_element_type=jnp.float32,
        )
        return ((key_sum, value_sum), query_grad)

    zero_block = jnp.zeros(keys_split.shape, jnp.float32)
    (key_sum, value_sum), query_grads = lax.scan(
        one_block, (zero_block, zero_block), (query_blocks, grad_blocks, logsum)
    )
    return (
        query_grads.reshape(queries.shape),
        key_sum.reshape(queries.shape),
        value_sum.reshape(queries.shape),
    )


def flip(array_in, axis_name, bits):
    size = lax.axis_size(axis_name)
    return lax.ppermute(array_in, axis_name, [(i, i ^ bits) for i in range(size)])


def total(array_in, axis_names):
    for name in axis_names:
        bits = 1
        while bits < lax.axis_size(name):
            array_in = array_in + flip(array_in, name, bits)
            bits *= 2
    return array_in


def shards(
    hidden_in,
    lengths,
    query_weight,
    query_bias,
    key_weight,
    value_weight,
    value_bias,
    output_weight,
    output_bias,
    first_gain,
    first_shift,
    inner_weight,
    inner_bias,
    outer_weight,
    outer_bias,
    second_gain,
    second_shift,
    cotangent,
    teacher,
):
    seq_len, model_width = hidden_in.shape
    ranks = lax.axis_size("tensor")
    rank = lax.axis_index("tensor")
    copies = lax.axis_size("dp")
    copy = lax.axis_index("dp")
    share_rows = seq_len // ranks
    heads_width = query_weight.shape[1]
    units = inner_weight.shape[1]
    score_scale = 1.0 / math.sqrt(HD)
    row_valid = jnp.arange(seq_len, dtype=jnp.int32) < lengths[0]

    def take_own(array_in):
        return lax.dynamic_slice_in_dim(array_in, rank * share_rows, share_rows, 0)

    def gather(weight):
        rows = weight.shape[0] // copies
        part = lax.dynamic_slice_in_dim(weight, copy * rows, rows, 0)
        others = jnp.stack([flip(part, "tensor", s) for s in range(1, ranks)])
        others = lax.all_gather(others, "dp", axis=1, tiled=True)
        return [weight] + [others[s] for s in range(ranks - 1)]

    output_weights = gather(output_weight)
    inner_weights = gather(inner_weight)
    outer_weights = gather(outer_weight)
    inner_biases = [inner_bias] + [flip(inner_bias, "tensor", s) for s in range(1, ranks)]
    token_total = total(lengths, ("dp",))[0].astype(jnp.float32)
    grad_scale = seq_len * copies / (2.0 * token_total)

    def spread(array_in):
        own = []
        for s in range(ranks):
            start = (rank ^ s) * share_rows
            own.append(lax.dynamic_slice_in_dim(array_in, start, share_rows, 0))
        return own

    def exchange(blocks):
        return [blocks[0]] + [flip(blocks[s], "tensor", s) for s in range(1, ranks)]

    queries = (matmul(hidden_in, query_weight) + query_bias).astype(jnp.bfloat16)
    keys_all = matmul(hidden_in, key_weight).astype(jnp.bfloat16)
    values_all = (matmul(hidden_in, value_weight) + value_bias).astype(jnp.bfloat16)
    context, logsum = attend_forward(queries, keys_all, values_all, row_valid, score_scale)
    contexts = exchange(spread(context.astype(jnp.bfloat16)))

    hidden_own = take_own(hidden_in).astype(jnp.float32)
    attention = sum(times_rows(c, w) for c, w in zip(contexts, output_weights))
    normed, normal_one, inverse_one = layer_norm(
        hidden_own + (attention + output_bias), first_gain, first_shift
    )
    normed_low = normed.astype(jnp.bfloat16)
    activated, slopes = [], []
    branch = outer_bias.astype(jnp.float32)
    for s in range(ranks):
        value, slope = gelu_parts(matmul(normed_low, inner_weights[s]) + inner_biases[s])
        activated.append(value.astype(jnp.bfloat16))
        slopes.append(slope.astype(jnp.bfloat16))
        branch = branch + times_rows(activated[s], outer_weights[s])
    final, normal_two, inverse_two = layer_norm(normed + branch, second_gain, second_shift)
    row_mask = take_own(row_valid)[:, None]
    difference = final - take_own(teacher).astype(jnp.float32)
    loss_part = jnp.sum(jnp.where(row_mask, difference * difference, 0.0))
    final_grad = jnp.where(
        row_mask, take_own(cotangent).astype(jnp.float32) + grad_scale * difference, 0.0
    )
    second_grad = norm_back(final_grad, normal_two, inverse_two, second_gain)
    branch_low = second_grad.astype(jnp.bfloat16)
    inner_lows = []
    normed_grad = second_grad
    for s in range(ranks):
        inner_low = (matmul(branch_low, outer_weights[s]) * slopes[s]).astype(jnp.bfloat16)
        inner_lows.append(inner_low)
        normed_grad = normed_grad + times_rows(inner_low, inner_weights[s])
    first_grad = norm_back(normed_grad, normal_one, inverse_one, first_gain)
    attention_low = first_grad.astype(jnp.bfloat16)
    grads = exchange([matmul(attention_low, w).astype(jnp.bfloat16) for w in output_weights])
    context_grad = jnp.zeros((seq_len, heads_width), jnp.bfloat16)
    for s in range(ranks):
        context_grad = lax.dynamic_update_slice_in_dim(
            context_grad, grads[s], (rank ^ s) * share_rows, 0
        )

    def reduce(former, latter):
        whole = over_rows(former, latter).astype(jnp.bfloat16)
        rows = lax.psum_scatter(whole, "dp", scatter_dimension=0, tiled=True)
        return sum(g.astype(jnp.float32) for g in exchange(jnp.split(rows, ranks, axis=1)))

    activated_all = jnp.concatenate(activated, axis=1)
    inner_low_all = jnp.concatenate(inner_lows, axis=1)
    outer_weight_grad = reduce(branch_low, activated_all)
    inner_weight_grad = reduce(normed_low, inner_low_all)
    output_weight_grad = reduce(attention_low, jnp.concatenate(contexts, axis=1))

    query_grad, key_grad, value_grad = attend_backward(
        queries, keys_all, values_all, row_valid, score_scale, logsum, context_grad
    )
    query_low = query_grad.astype(jnp.bfloat16)
    key_low = key_grad.astype(jnp.bfloat16)
    value_low = value_grad.astype(jnp.bfloat16)
    input_part = (
        times_rows(query_low, query_weight)
        + times_rows(key_low, key_weight)
        + times_rows(value_low, value_weight)
    )
    input_rows = first_grad + lax.psum_scatter(
        input_part.astype(jnp.bfloat16), "tensor", scatter_dimension=0, tiled=True
    ).astype(jnp.float32)
    qkv_low = jnp.concatenate([query_low, key_low, value_low], axis=1)
    qkv_sum = lax.psum_scatter(
        over_rows(hidden_in, qkv_low).astype(jnp.bfloat16), "dp", scatter_dimension=0, tiled=True
    ).astype(jnp.float32)
    query_weight_grad, key_weight_grad, value_weight_grad = jnp.split(qkv_sum, 3, axis=1)

    def column_sums(array_in):
        return jnp.sum(array_in.astype(jnp.float32), axis=0)

    def placed(vector_in):
        zeros = jnp.zeros((vector_in.shape[0] * ranks,), jnp.float32)
        return lax.dynamic_update_slice_in_dim(zeros, vector_in, rank * vector_in.shape[0], 0)

    inner_sums = column_sums(inner_low_all).reshape(ranks, units)
    inner_sums = jnp.concatenate(
        [lax.dynamic_index_in_dim(inner_sums, rank ^ s, 0, keepdims=False) for s in range(ranks)]
    )
    vectors = [
        inner_sums,
        column_sums(attention_low),
        column_sums(normed_grad * normal_one),
        column_sums(normed_grad),
        column_sums(branch_low),
        column_sums(final_grad * normal_two),
        column_sums(final_grad),
        jnp.full((model_width,), loss_part),
    ]
    vectors = total(jnp.concatenate(vectors).reshape(-1, model_width), ("dp", "tensor"))
    late = jnp.stack([placed(column_sums(query_low)), placed(column_sums(value_low))])
    late = total(late, ("dp", "tensor"))
    wide = inner_sums.shape[0] // model_width
    inner_bias_grad = vectors[:wide].reshape(-1)
    (
        output_bias_grad,
        first_gain_grad,
        first_shift_grad,
        outer_bias_grad,
        second_gain_grad,
        second_shift_grad,
    ) = [vectors[wide + i] for i in range(6)]
    return (
        final.astype(jnp.bfloat16),
        vectors[wide + 6, 0] / token_total,
        input_rows,
        query_weight_grad,
        late[0],
        key_weight_grad,
        value_weight_grad,
        late[1],
        output_weight_grad,
        output_bias_grad,
        first_gain_grad,
        first_shift_grad,
        inner_weight_grad,
        inner_bias_grad,
        outer_weight_grad,
        outer_bias_grad,
        second_gain_grad,
        second_shift_grad,
    )


def solution(mesh):
    rows, columns, split = P("dp", None), P(None, "tensor"), P("dp", "tensor")
    part, whole, own = P("tensor"), P(), P(("dp", "tensor"), None)
    in_specs = (
        rows,
        P("dp"),
        columns,
        part,
        columns,
        columns,
        part,
        columns,
        whole,
        whole,
        whole,
        columns,
        part,
        columns,
        whole,
        whole,
        whole,
        rows,
        rows,
    )
    out_specs = (
        own,
        whole,
        own,
        split,
        whole,
        split,
        split,
        whole,
        split,
        whole,
        whole,
        whole,
        split,
        whole,
        split,
        whole,
        whole,
        whole,
    )
    return jax.shard_map(shards, mesh=mesh, in_specs=in_specs, out_specs=out_specs, check_vma=False)
```

```python
import jax
import jax.numpy as jnp
from jax import lax
from jax.experimental import pallas as pl
from jax.experimental.pallas import tpu as pltpu
from jax.sharding import PartitionSpec as P

HD = 64
PAIR = 128
VMEM_BYTES = 60000 * 1024


epsilon = 1e-05


def matmul(former, latter):
    return jnp.dot(former, latter, preferred_element_type=jnp.float32)


def times_rows(former, latter):
    return lax.dot_general(
        former, latter, (((1,), (1,)), ((), ())), preferred_element_type=jnp.float32
    )


def over_rows(former, latter):
    return lax.dot_general(
        former, latter, (((0,), (0,)), ((), ())), preferred_element_type=jnp.float32
    )


def layer_norm(hidden, norm_gain, norm_shift):
    centered = hidden - jnp.mean(hidden, axis=-1, keepdims=True)
    inverse = lax.rsqrt(jnp.mean(centered * centered, axis=-1, keepdims=True) + epsilon)
    normal = centered * inverse
    return (normal * norm_gain + norm_shift, normal, inverse)


def norm_back(upstream, normal, inverse, norm_gain):
    scaled = upstream * norm_gain
    return inverse * (
        scaled
        - jnp.mean(scaled, axis=-1, keepdims=True)
        - normal * jnp.mean(scaled * normal, axis=-1, keepdims=True)
    )


def gelu_parts(values):
    cumulative = 0.5 * (1.0 + jax.scipy.special.erf(values * 0.7071067811865476))
    slope = cumulative + values * jnp.exp(-0.5 * values * values) * 0.3989422804014327
    return (values * cumulative, slope)


def lanes(rows):
    return lax.broadcasted_iota(jnp.int32, (rows, PAIR), 1)


def in_head(lane, head):
    return (lane < HD) if head == 0 else (lane >= HD)


def extend(base, lane, head, first, offset):
    start = HD * (1 - head)
    high = offset.astype(jnp.bfloat16).astype(jnp.float32)
    middle = (offset - high).astype(jnp.bfloat16).astype(jnp.float32)
    out = jnp.where(lane == start, first, 0.0)
    out = jnp.where(lane == start + 1, -high, out)
    out = jnp.where(lane == start + 2, -middle, out)
    out = jnp.where(lane == start + 3, high + middle - offset, out)
    return jnp.where(in_head(lane, head), base, out).astype(jnp.bfloat16)


def extend_keys(keys, lane, head, row_start, length):
    start = HD * (1 - head)
    position = row_start + lax.broadcasted_iota(jnp.int32, keys.shape, 0)
    bias = jnp.where(position < length, 0.0, -1e30)
    ones = jnp.where((lane > start) & (lane < start + 4), 1.0, 0.0)
    side = jnp.where(lane == start, bias, ones)
    return jnp.where(in_head(lane, head), keys, side).astype(jnp.bfloat16)


def extend_values(values, lane, head):
    return jnp.where(in_head(lane, head), values, 1.0).astype(jnp.bfloat16)


def forward_kernel(length_ref, q_ref, k_ref, v_ref, context_ref, extended_ref, keys, values):
    @pl.when(pl.program_id(0) == 0)
    def _():
        lane = lanes(k_ref.shape[0])
        k_float = k_ref[...].astype(jnp.float32)
        v_float = v_ref[...].astype(jnp.float32)
        for head in range(2):
            keys[head] = extend_keys(k_float, lane, head, 0, length_ref[0])
            values[head] = extend_values(v_float, lane, head)

    lane = lanes(q_ref.shape[0])
    scaled = q_ref[...].astype(jnp.float32) * HD**-0.5
    contexts = []
    for head in range(2):
        plain = jnp.where(lane == HD * (1 - head), 1.0, 0.0)
        query = jnp.where(in_head(lane, head), scaled, plain).astype(jnp.bfloat16)
        scores = times_rows(query, keys[head])
        peak = jnp.max(scores, axis=1, keepdims=True)
        exponent = jnp.exp(scores - peak).astype(jnp.bfloat16)
        out = matmul(exponent, values[head])
        contexts.append(out / pltpu.roll(out, HD, 1))
        extended_ref[head] = extend(scaled, lane, head, 1.0, peak + jnp.log(out))
    context_ref[...] = jnp.where(lane < HD, contexts[0], contexts[1]).astype(jnp.bfloat16)


def attend_forward(length, qkv, pair):
    seq_len = qkv.shape[0]
    rows = min(256, seq_len)
    return pl.pallas_call(
        forward_kernel,
        grid_spec=pltpu.PrefetchScalarGridSpec(
            num_scalar_prefetch=1,
            grid=(seq_len // rows,),
            in_specs=[
                pl.BlockSpec((rows, PAIR), lambda i, n: (i, 3 * pair)),
                pl.BlockSpec((seq_len, PAIR), lambda i, n: (0, 3 * pair + 1)),
                pl.BlockSpec((seq_len, PAIR), lambda i, n: (0, 3 * pair + 2)),
            ],
            out_specs=[
                pl.BlockSpec((rows, PAIR), lambda i, n: (i, 0)),
                pl.BlockSpec((2, rows, PAIR), lambda i, n: (0, i, 0)),
            ],
            scratch_shapes=[pltpu.VMEM((2, seq_len, PAIR), jnp.bfloat16)] * 2,
        ),
        out_shape=[
            jax.ShapeDtypeStruct((seq_len, PAIR), jnp.bfloat16),
            jax.ShapeDtypeStruct((2, seq_len, PAIR), jnp.bfloat16),
        ],
        compiler_params=pltpu.CompilerParams(vmem_limit_bytes=VMEM_BYTES),
        cost_estimate=pl.CostEstimate(
            flops=8 * seq_len * seq_len * 2 * PAIR,
            bytes_accessed=12 * seq_len * PAIR,
            transcendentals=2 * seq_len * seq_len,
        ),
        name="attend_forward",
    )(length, qkv, qkv, qkv)


def backward_kernel(length_ref, extended_ref, k_ref, v_ref, context_ref, grad_ref, out_ref, grads, turned):
    step = pl.program_id(0)
    seq_len, rows = grad_ref.shape[0], k_ref.shape[0]

    @pl.when(step == 0)
    def _():
        def prepare(j, carry):
            here = pl.ds(pl.multiple_of(j * rows, rows), rows)
            lane = lanes(rows)
            grad = grad_ref[here, :].astype(jnp.float32)
            product = grad * context_ref[here, :].astype(jnp.float32)
            for head in range(2):
                centre = jnp.sum(
                    jnp.where(in_head(lane, head), product, 0.0), axis=1, keepdims=True
                )
                grads[head, here, :] = extend(grad, lane, head, 0.0, centre)
            return carry

        lax.fori_loop(0, seq_len // rows, prepare, 0)

    lane = lanes(rows)
    k_float = k_ref[...].astype(jnp.float32)
    v_float = v_ref[...].astype(jnp.float32)
    across = k_float.T.astype(jnp.bfloat16)
    key_grads, value_grads = [], []
    for head in range(2):
        keys = extend_keys(k_float, lane, head, step * rows, length_ref[0])
        values = extend_values(v_float, lane, head)
        query, grad = extended_ref[head], grads[head]
        probs = jnp.exp(times_rows(keys, query))
        score_grad = (probs * times_rows(values, grad)).astype(jnp.bfloat16)
        value_grads.append(matmul(probs.astype(jnp.bfloat16), grad))
        key_grads.append(matmul(score_grad, query))
        own = slice(HD * head, HD * (head + 1))
        part = matmul(across[own], score_grad)

        @pl.when(step == 0)
        def _():
            turned[own, :] = part

        @pl.when(step > 0)
        def _():
            turned[own, :] += part

    here = pl.ds(pl.multiple_of(step * rows, rows), rows)
    key_grad = jnp.where(lane < HD, key_grads[0], key_grads[1])
    value_grad = jnp.where(lane < HD, value_grads[0], value_grads[1])
    out_ref[here, PAIR : 2 * PAIR] = key_grad.astype(jnp.bfloat16)
    out_ref[here, 2 * PAIR :] = value_grad.astype(jnp.bfloat16)

    @pl.when(step == pl.num_programs(0) - 1)
    def _():
        def finish(j, carry):
            here = pl.ds(pl.multiple_of(j * rows, rows), rows)
            out_ref[here, :PAIR] = (turned[:, here].T * HD**-0.5).astype(jnp.bfloat16)
            return carry

        lax.fori_loop(0, seq_len // rows, finish, 0)


def attend_backward(length, extended, qkv, context, context_grad, pair):
    seq_len = qkv.shape[0]
    rows = min(256, seq_len)
    return pl.pallas_call(
        backward_kernel,
        grid_spec=pltpu.PrefetchScalarGridSpec(
            num_scalar_prefetch=1,
            grid=(seq_len // rows,),
            in_specs=[
                pl.BlockSpec((2, seq_len, PAIR), lambda i, n: (0, 0, 0)),
                pl.BlockSpec((rows, PAIR), lambda i, n: (i, 3 * pair + 1)),
                pl.BlockSpec((rows, PAIR), lambda i, n: (i, 3 * pair + 2)),
                pl.BlockSpec((seq_len, PAIR), lambda i, n: (0, 0)),
                pl.BlockSpec((seq_len, PAIR), lambda i, n: (0, pair)),
            ],
            out_specs=pl.BlockSpec((seq_len, 3 * PAIR), lambda i, n: (0, 0)),
            scratch_shapes=[
                pltpu.VMEM((2, seq_len, PAIR), jnp.bfloat16),
                pltpu.VMEM((PAIR, seq_len), jnp.float32),
            ],
        ),
        out_shape=jax.ShapeDtypeStruct((seq_len, 3 * PAIR), jnp.bfloat16),
        compiler_params=pltpu.CompilerParams(vmem_limit_bytes=VMEM_BYTES),
        cost_estimate=pl.CostEstimate(
            flops=20 * seq_len * seq_len * 2 * PAIR,
            bytes_accessed=20 * seq_len * PAIR,
            transcendentals=2 * seq_len * seq_len,
        ),
        name="attend_backward",
    )(length, extended, qkv, qkv, context, context_grad)


def flip(array_in, axis_name, bits):
    size = lax.axis_size(axis_name)
    return lax.ppermute(array_in, axis_name, [(i, i ^ bits) for i in range(size)])


def total(array_in, axis_names):
    for name in axis_names:
        bits = 1
        while bits < lax.axis_size(name):
            array_in = array_in + flip(array_in, name, bits)
            bits *= 2
    return array_in


def shards(
    hidden_in,
    lengths,
    query_weight,
    query_bias,
    key_weight,
    value_weight,
    value_bias,
    output_weight,
    output_bias,
    first_gain,
    first_shift,
    inner_weight,
    inner_bias,
    outer_weight,
    outer_bias,
    second_gain,
    second_shift,
    cotangent,
    teacher,
):
    seq_len, model_width = hidden_in.shape
    ranks = lax.axis_size("tensor")
    rank = lax.axis_index("tensor")
    copies = lax.axis_size("dp")
    copy = lax.axis_index("dp")
    share_rows = seq_len // ranks
    heads_width = query_weight.shape[1]
    units = inner_weight.shape[1]
    pairs = heads_width // PAIR
    row_valid = jnp.arange(seq_len, dtype=jnp.int32) < lengths[0]

    def take_own(array_in):
        return lax.dynamic_slice_in_dim(array_in, rank * share_rows, share_rows, 0)

    def by_pairs(*arrays):
        return jnp.concatenate(
            [a[..., p * PAIR : (p + 1) * PAIR] for p in range(pairs) for a in arrays], axis=-1
        )

    qkv_weight = by_pairs(query_weight, key_weight, value_weight)
    qkv_bias = by_pairs(query_bias, jnp.zeros_like(query_bias), value_bias)

    def gather(weight):
        rows = weight.shape[0] // copies
        part = lax.dynamic_slice_in_dim(weight, copy * rows, rows, 0)
        others = jnp.stack([flip(part, "tensor", s) for s in range(1, ranks)])
        others = lax.all_gather(others, "dp", axis=1, tiled=True)
        return [weight] + [others[s] for s in range(ranks - 1)]

    def spread(array_in):
        own = []
        for s in range(ranks):
            start = (rank ^ s) * share_rows
            own.append(lax.dynamic_slice_in_dim(array_in, start, share_rows, 0))
        return own

    def exchange(blocks):
        return [blocks[0]] + [flip(blocks[s], "tensor", s) for s in range(1, ranks)]

    def ordered(vector_in):
        table = vector_in.reshape(ranks, -1)
        return jnp.concatenate(
            [lax.dynamic_index_in_dim(table, rank ^ s, 0, keepdims=False) for s in range(ranks)]
        )

    early = gather(jnp.concatenate([inner_weight, output_weight], axis=1))
    inner_weights = [w[:, :units] for w in early]
    output_weight_all = jnp.concatenate([w[:, units:] for w in early], axis=1)
    outer_weights = gather(outer_weight)
    qkv_weights = gather(qkv_weight)
    inner_biases = [inner_bias] + [flip(inner_bias, "tensor", s) for s in range(1, ranks)]
    token_total = total(lengths, ("dp",))[0].astype(jnp.float32)
    grad_scale = seq_len * copies / (2.0 * token_total)

    qkv = (matmul(hidden_in, qkv_weight) + qkv_bias).astype(jnp.bfloat16)
    contexts, extended, received = [], [], []
    for pair in range(pairs):
        context, queries = attend_forward(lengths, qkv, pair)
        contexts.append(context)
        extended.append(queries)
        received.append(exchange(spread(context)))
    context_all = jnp.concatenate([received[p][s] for s in range(ranks) for p in range(pairs)], axis=1)

    hidden_own = take_own(hidden_in).astype(jnp.float32)
    attention = times_rows(context_all, output_weight_all)
    normed, normal_one, inverse_one = layer_norm(
        hidden_own + (attention + output_bias), first_gain, first_shift
    )
    normed_low = normed.astype(jnp.bfloat16)
    activated, slopes = [], []
    branch = outer_bias.astype(jnp.float32)
    for s in range(ranks):
        value, slope = gelu_parts(matmul(normed_low, inner_weights[s]) + inner_biases[s])
        activated.append(value.astype(jnp.bfloat16))
        slopes.append(slope.astype(jnp.bfloat16))
        branch = branch + times_rows(activated[s], outer_weights[s])
    final, normal_two, inverse_two = layer_norm(normed + branch, second_gain, second_shift)
    row_mask = take_own(row_valid)[:, None]
    difference = final - take_own(teacher).astype(jnp.float32)
    loss_part = jnp.sum(jnp.where(row_mask, difference * difference, 0.0))
    final_grad = jnp.where(
        row_mask, take_own(cotangent).astype(jnp.float32) + grad_scale * difference, 0.0
    )
    second_grad = norm_back(final_grad, normal_two, inverse_two, second_gain)
    branch_low = second_grad.astype(jnp.bfloat16)
    outer_whole = over_rows(branch_low, jnp.concatenate(activated, axis=1)).astype(jnp.bfloat16)
    inner_lows = []
    normed_grad = second_grad
    for s in range(ranks):
        inner_low = (matmul(branch_low, outer_weights[s]) * slopes[s]).astype(jnp.bfloat16)
        inner_lows.append(inner_low)
        normed_grad = normed_grad + times_rows(inner_low, inner_weights[s])
    first_grad = norm_back(normed_grad, normal_one, inverse_one, first_gain)
    attention_low = first_grad.astype(jnp.bfloat16)
    grad_all = matmul(attention_low, output_weight_all).astype(jnp.bfloat16)
    grads = exchange(jnp.split(grad_all, ranks, axis=1))
    context_grad = jnp.zeros((seq_len, heads_width), jnp.bfloat16)
    for s in range(ranks):
        context_grad = lax.dynamic_update_slice_in_dim(
            context_grad, grads[s], (rank ^ s) * share_rows, 0
        )

    inner_low_all = jnp.concatenate(inner_lows, axis=1)
    inner_whole = over_rows(normed_low, inner_low_all).astype(jnp.bfloat16)
    output_whole = over_rows(attention_low, context_all).astype(jnp.bfloat16)

    def reduce_copies(whole):
        rows = whole.shape[0] // copies
        bits = [1]
        while 2 * bits[0] < copies:
            bits.insert(0, 2 * bits[0])
        bits = [1] + bits[:-1]
        blocks = whole.reshape(copies, rows, -1)
        left = list(range(copies.bit_length() - 1))
        for bit in bits:
            place = bit.bit_length() - 1
            low = 1
            for p in left:
                low *= 2 if p < place else 1
            left.remove(place)
            blocks = blocks.reshape(-1, 2, low, rows, blocks.shape[-1])
            mine = (copy >> place) & 1
            keep = lax.dynamic_index_in_dim(blocks, mine, 1, keepdims=False)
            give = lax.dynamic_index_in_dim(blocks, 1 - mine, 1, keepdims=False)
            come = flip(give, "dp", bit)
            blocks = (keep.astype(jnp.float32) + come.astype(jnp.float32)).astype(jnp.bfloat16)
            blocks = blocks.reshape(-1, rows, blocks.shape[-1])
        return blocks[0]

    def scatter_copies(whole):
        return lax.psum_scatter(whole, "dp", scatter_dimension=0, tiled=True)

    def reduce_ranks(blocks):
        return sum(g.astype(jnp.float32) for g in exchange(blocks))

    context_grad, outer_whole, inner_whole, output_whole = lax.optimization_barrier(
        (context_grad, outer_whole, inner_whole, output_whole)
    )
    outer_rows = scatter_copies(outer_whole)
    outer_weight_grad = reduce_ranks(jnp.split(outer_rows, ranks, axis=1))
    both_rows = reduce_copies(jnp.concatenate([inner_whole, output_whole], axis=1))
    inner_rows = jnp.split(both_rows[:, : ranks * units], ranks, axis=1)
    output_rows = jnp.split(both_rows[:, ranks * units :], ranks, axis=1)
    both_sum = reduce_ranks(
        [jnp.concatenate([i, o], axis=1) for i, o in zip(inner_rows, output_rows)]
    )
    inner_weight_grad, output_weight_grad = both_sum[:, :units], both_sum[:, units:]

    input_rows = first_grad
    qkv_sums, query_sums = [], []
    for pair in range(pairs):
        qkv_low = attend_backward(lengths, extended[pair], qkv, contexts[pair], context_grad, pair)
        columns = slice(3 * PAIR * pair, 3 * PAIR * (pair + 1))
        for block, weight in zip(exchange(spread(qkv_low)), qkv_weights):
            input_rows = input_rows + times_rows(block, weight[:, columns])
        whole = over_rows(hidden_in, qkv_low).astype(jnp.bfloat16)
        qkv_sums.append(scatter_copies(whole) if pair == 0 else reduce_copies(whole))
        query_sums.append(jnp.sum(qkv_low[:, :PAIR].astype(jnp.float32), axis=0))
    qkv_sums = [jnp.split(w.astype(jnp.float32), 3, axis=1) for w in qkv_sums]
    query_weight_grad, key_weight_grad, value_weight_grad = [
        jnp.concatenate([w[i] for w in qkv_sums], axis=1) for i in range(3)
    ]

    def column_sums(array_in):
        return jnp.sum(array_in.astype(jnp.float32), axis=0)

    vectors = [
        ordered(column_sums(inner_low_all)),
        column_sums(attention_low),
        column_sums(normed_grad * normal_one),
        column_sums(normed_grad),
        column_sums(branch_low),
        column_sums(final_grad * normal_two),
        column_sums(final_grad),
        ordered(column_sums(grad_all)),
        jnp.full((model_width,), loss_part),
    ]
    vectors = jnp.concatenate(vectors).reshape(-1, model_width)
    vectors = jnp.sum(lax.all_gather(vectors, ("dp", "tensor")), axis=0)
    wide = ranks * units // model_width
    inner_bias_grad = vectors[:wide].reshape(-1)
    (
        output_bias_grad,
        first_gain_grad,
        first_shift_grad,
        outer_bias_grad,
        second_gain_grad,
        second_shift_grad,
        value_bias_grad,
    ) = [vectors[wide + i] for i in range(7)]
    query_bias_grad = lax.dynamic_update_slice_in_dim(
        jnp.zeros((model_width,), jnp.float32), jnp.concatenate(query_sums), rank * heads_width, 0
    )
    query_bias_grad = total(query_bias_grad, ("dp", "tensor"))
    return (
        final.astype(jnp.bfloat16),
        vectors[wide + 7, 0] / token_total,
        input_rows,
        query_weight_grad,
        query_bias_grad,
        key_weight_grad,
        value_weight_grad,
        value_bias_grad,
        output_weight_grad,
        output_bias_grad,
        first_gain_grad,
        first_shift_grad,
        inner_weight_grad,
        inner_bias_grad,
        outer_weight_grad,
        outer_bias_grad,
        second_gain_grad,
        second_shift_grad,
    )


def solution(mesh):
    rows, columns, split = P("dp", None), P(None, "tensor"), P("dp", "tensor")
    part, whole, own = P("tensor"), P(), P(("dp", "tensor"), None)
    in_specs = (
        rows,
        P("dp"),
        columns,
        part,
        columns,
        columns,
        part,
        columns,
        whole,
        whole,
        whole,
        columns,
        part,
        columns,
        whole,
        whole,
        whole,
        rows,
        rows,
    )
    out_specs = (
        own,
        whole,
        own,
        split,
        whole,
        split,
        split,
        whole,
        split,
        whole,
        whole,
        whole,
        split,
        whole,
        split,
        whole,
        whole,
        whole,
    )
    return jax.shard_map(shards, mesh=mesh, in_specs=in_specs, out_specs=out_specs, check_vma=False)
```

```python
import jax
import jax.numpy as jnp
from jax import lax
from jax.experimental import pallas as pl
from jax.experimental.pallas import tpu as pltpu
from jax.sharding import PartitionSpec as P

HD = 64
PAIR = 128
VMEM_BYTES = 60000 * 1024


epsilon = 1e-05


def matmul(former, latter):
    return jnp.dot(former, latter, preferred_element_type=jnp.float32)


def times_rows(former, latter):
    return lax.dot_general(
        former, latter, (((1,), (1,)), ((), ())), preferred_element_type=jnp.float32
    )


def over_rows(former, latter):
    return lax.dot_general(
        former, latter, (((0,), (0,)), ((), ())), preferred_element_type=jnp.float32
    )


def layer_norm(hidden, norm_gain, norm_shift):
    centered = hidden - jnp.mean(hidden, axis=-1, keepdims=True)
    inverse = lax.rsqrt(jnp.mean(centered * centered, axis=-1, keepdims=True) + epsilon)
    normal = centered * inverse
    return (normal * norm_gain + norm_shift, normal, inverse)


def norm_back(upstream, normal, inverse, norm_gain):
    scaled = upstream * norm_gain
    return inverse * (
        scaled
        - jnp.mean(scaled, axis=-1, keepdims=True)
        - normal * jnp.mean(scaled * normal, axis=-1, keepdims=True)
    )


def gelu_parts(values):
    cumulative = 0.5 * (1.0 + jax.scipy.special.erf(values * 0.7071067811865476))
    slope = cumulative + values * jnp.exp(-0.5 * values * values) * 0.3989422804014327
    return (values * cumulative, slope)


def lanes(rows):
    return lax.broadcasted_iota(jnp.int32, (rows, PAIR), 1)


def in_head(lane, head):
    return (lane < HD) if head == 0 else (lane >= HD)


def extend(base, lane, head, first, offset):
    start = HD * (1 - head)
    high = offset.astype(jnp.bfloat16).astype(jnp.float32)
    middle = (offset - high).astype(jnp.bfloat16).astype(jnp.float32)
    out = jnp.where(lane == start, first, 0.0)
    out = jnp.where(lane == start + 1, -high, out)
    out = jnp.where(lane == start + 2, -middle, out)
    out = jnp.where(lane == start + 3, high + middle - offset, out)
    return jnp.where(in_head(lane, head), base, out).astype(jnp.bfloat16)


def extend_keys(keys, lane, head, row_start, length):
    start = HD * (1 - head)
    position = row_start + lax.broadcasted_iota(jnp.int32, keys.shape, 0)
    bias = jnp.where(position < length, 0.0, -1e30)
    ones = jnp.where((lane > start) & (lane < start + 4), 1.0, 0.0)
    side = jnp.where(lane == start, bias, ones)
    return jnp.where(in_head(lane, head), keys, side).astype(jnp.bfloat16)


def extend_values(values, lane, head):
    return jnp.where(in_head(lane, head), values, 1.0).astype(jnp.bfloat16)


def forward_kernel(length_ref, q_ref, k_ref, v_ref, context_ref, extended_ref, keys, values):
    @pl.when(pl.program_id(0) == 0)
    def _():
        lane = lanes(k_ref.shape[0])
        k_float = k_ref[...].astype(jnp.float32)
        v_float = v_ref[...].astype(jnp.float32)
        for head in range(2):
            keys[head] = extend_keys(k_float, lane, head, 0, length_ref[0])
            values[head] = extend_values(v_float, lane, head)

    lane = lanes(q_ref.shape[0])
    scaled = q_ref[...].astype(jnp.float32) * HD**-0.5
    contexts = []
    for head in range(2):
        plain = jnp.where(lane == HD * (1 - head), 1.0, 0.0)
        query = jnp.where(in_head(lane, head), scaled, plain).astype(jnp.bfloat16)
        scores = times_rows(query, keys[head])
        peak = jnp.max(scores, axis=1, keepdims=True)
        exponent = jnp.exp(scores - peak).astype(jnp.bfloat16)
        out = matmul(exponent, values[head])
        contexts.append(out / pltpu.roll(out, HD, 1))
        extended_ref[head] = extend(scaled, lane, head, 1.0, peak + jnp.log(out))
    context_ref[...] = jnp.where(lane < HD, contexts[0], contexts[1]).astype(jnp.bfloat16)


def attend_forward(length, qkv, pair):
    seq_len = qkv.shape[0]
    rows = min(256, seq_len)
    return pl.pallas_call(
        forward_kernel,
        grid_spec=pltpu.PrefetchScalarGridSpec(
            num_scalar_prefetch=1,
            grid=(seq_len // rows,),
            in_specs=[
                pl.BlockSpec((rows, PAIR), lambda i, n: (i, 3 * pair)),
                pl.BlockSpec((seq_len, PAIR), lambda i, n: (0, 3 * pair + 1)),
                pl.BlockSpec((seq_len, PAIR), lambda i, n: (0, 3 * pair + 2)),
            ],
            out_specs=[
                pl.BlockSpec((rows, PAIR), lambda i, n: (i, 0)),
                pl.BlockSpec((2, rows, PAIR), lambda i, n: (0, i, 0)),
            ],
            scratch_shapes=[pltpu.VMEM((2, seq_len, PAIR), jnp.bfloat16)] * 2,
        ),
        out_shape=[
            jax.ShapeDtypeStruct((seq_len, PAIR), jnp.bfloat16),
            jax.ShapeDtypeStruct((2, seq_len, PAIR), jnp.bfloat16),
        ],
        compiler_params=pltpu.CompilerParams(vmem_limit_bytes=VMEM_BYTES),
        cost_estimate=pl.CostEstimate(
            flops=8 * seq_len * seq_len * 2 * PAIR,
            bytes_accessed=12 * seq_len * PAIR,
            transcendentals=2 * seq_len * seq_len,
        ),
        name="attend_forward",
    )(length, qkv, qkv, qkv)


def backward_kernel(length_ref, extended_ref, k_ref, v_ref, context_ref, grad_ref, out_ref, grads, turned):
    step = pl.program_id(0)
    seq_len, rows = grad_ref.shape[0], k_ref.shape[0]

    @pl.when(step == 0)
    def _():
        def prepare(j, carry):
            here = pl.ds(pl.multiple_of(j * rows, rows), rows)
            lane = lanes(rows)
            grad = grad_ref[here, :].astype(jnp.float32)
            product = grad * context_ref[here, :].astype(jnp.float32)
            for head in range(2):
                centre = jnp.sum(
                    jnp.where(in_head(lane, head), product, 0.0), axis=1, keepdims=True
                )
                grads[head, here, :] = extend(grad, lane, head, 0.0, centre)
            return carry

        lax.fori_loop(0, seq_len // rows, prepare, 0)

    lane = lanes(rows)
    k_float = k_ref[...].astype(jnp.float32)
    v_float = v_ref[...].astype(jnp.float32)
    across = k_float.T.astype(jnp.bfloat16)
    key_grads, value_grads = [], []
    for head in range(2):
        keys = extend_keys(k_float, lane, head, step * rows, length_ref[0])
        values = extend_values(v_float, lane, head)
        query, grad = extended_ref[head], grads[head]
        probs = jnp.exp(times_rows(keys, query))
        score_grad = (probs * times_rows(values, grad)).astype(jnp.bfloat16)
        value_grads.append(matmul(probs.astype(jnp.bfloat16), grad))
        key_grads.append(matmul(score_grad, query))
        own = slice(HD * head, HD * (head + 1))
        part = matmul(across[own], score_grad)

        @pl.when(step == 0)
        def _():
            turned[own, :] = part

        @pl.when(step > 0)
        def _():
            turned[own, :] += part

    here = pl.ds(pl.multiple_of(step * rows, rows), rows)
    key_grad = jnp.where(lane < HD, key_grads[0], key_grads[1])
    value_grad = jnp.where(lane < HD, value_grads[0], value_grads[1])
    out_ref[here, PAIR : 2 * PAIR] = key_grad.astype(jnp.bfloat16)
    out_ref[here, 2 * PAIR :] = value_grad.astype(jnp.bfloat16)

    @pl.when(step == pl.num_programs(0) - 1)
    def _():
        def finish(j, carry):
            here = pl.ds(pl.multiple_of(j * rows, rows), rows)
            out_ref[here, :PAIR] = (turned[:, here].T * HD**-0.5).astype(jnp.bfloat16)
            return carry

        lax.fori_loop(0, seq_len // rows, finish, 0)


def attend_backward(length, extended, qkv, context, context_grad, pair):
    seq_len = qkv.shape[0]
    rows = min(256, seq_len)
    return pl.pallas_call(
        backward_kernel,
        grid_spec=pltpu.PrefetchScalarGridSpec(
            num_scalar_prefetch=1,
            grid=(seq_len // rows,),
            in_specs=[
                pl.BlockSpec((2, seq_len, PAIR), lambda i, n: (0, 0, 0)),
                pl.BlockSpec((rows, PAIR), lambda i, n: (i, 3 * pair + 1)),
                pl.BlockSpec((rows, PAIR), lambda i, n: (i, 3 * pair + 2)),
                pl.BlockSpec((seq_len, PAIR), lambda i, n: (0, 0)),
                pl.BlockSpec((seq_len, PAIR), lambda i, n: (0, pair)),
            ],
            out_specs=pl.BlockSpec((seq_len, 3 * PAIR), lambda i, n: (0, 0)),
            scratch_shapes=[
                pltpu.VMEM((2, seq_len, PAIR), jnp.bfloat16),
                pltpu.VMEM((PAIR, seq_len), jnp.float32),
            ],
        ),
        out_shape=jax.ShapeDtypeStruct((seq_len, 3 * PAIR), jnp.bfloat16),
        compiler_params=pltpu.CompilerParams(vmem_limit_bytes=VMEM_BYTES),
        cost_estimate=pl.CostEstimate(
            flops=20 * seq_len * seq_len * 2 * PAIR,
            bytes_accessed=20 * seq_len * PAIR,
            transcendentals=2 * seq_len * seq_len,
        ),
        name="attend_backward",
    )(length, extended, qkv, qkv, context, context_grad)


def tie(*values):
    return lax.optimization_barrier(values)


def flip(array_in, axis_name, bits):
    size = lax.axis_size(axis_name)
    return lax.ppermute(array_in, axis_name, [(i, i ^ bits) for i in range(size)])


def total(array_in, axis_names):
    for name in axis_names:
        bits = 1
        while bits < lax.axis_size(name):
            array_in = array_in + flip(array_in, name, bits)
            bits *= 2
    return array_in


def shards(
    hidden_in,
    lengths,
    query_weight,
    query_bias,
    key_weight,
    value_weight,
    value_bias,
    output_weight,
    output_bias,
    first_gain,
    first_shift,
    inner_weight,
    inner_bias,
    outer_weight,
    outer_bias,
    second_gain,
    second_shift,
    cotangent,
    teacher,
):
    seq_len, model_width = hidden_in.shape
    ranks = lax.axis_size("tensor")
    rank = lax.axis_index("tensor")
    copies = lax.axis_size("dp")
    copy = lax.axis_index("dp")
    share_rows = seq_len // ranks
    heads_width = query_weight.shape[1]
    units = inner_weight.shape[1]
    pairs = heads_width // PAIR
    row_valid = jnp.arange(seq_len, dtype=jnp.int32) < lengths[0]

    def take_own(array_in):
        return lax.dynamic_slice_in_dim(array_in, rank * share_rows, share_rows, 0)

    def by_pairs(*arrays):
        return jnp.concatenate(
            [a[..., p * PAIR : (p + 1) * PAIR] for p in range(pairs) for a in arrays], axis=-1
        )

    def own_part(weight):
        rows = weight.shape[0] // copies
        return lax.dynamic_slice_in_dim(weight, copy * rows, rows, 0)

    def others(part):
        return jnp.stack([flip(part, "tensor", s) for s in range(1, ranks)])

    def gathered(parts):
        return lax.all_gather(parts, "dp", axis=1, tiled=True)

    def spread(array_in):
        own = []
        for s in range(ranks):
            start = (rank ^ s) * share_rows
            own.append(lax.dynamic_slice_in_dim(array_in, start, share_rows, 0))
        return own

    def exchange(blocks):
        return [blocks[0]] + [flip(blocks[s], "tensor", s) for s in range(1, ranks)]

    def reduce_ranks(blocks):
        return sum(g.astype(jnp.float32) for g in exchange(blocks))

    def ordered(vector_in):
        table = vector_in.reshape(ranks, -1)
        return jnp.concatenate(
            [lax.dynamic_index_in_dim(table, rank ^ s, 0, keepdims=False) for s in range(ranks)]
        )

    def half_columns(array_in, other):
        blocks = array_in.reshape(array_in.shape[0], copies // 2, 2, -1)
        mine = lax.dynamic_index_in_dim(blocks, (copy & 1) ^ other, 2, keepdims=False)
        return mine.reshape(array_in.shape[0], -1)

    def first_give(former, latter):
        return over_rows(half_columns(former, 1), latter).astype(jnp.bfloat16)

    def first_keep(former, latter, come):
        kept = over_rows(half_columns(former, 0), latter) + come.astype(jnp.float32)
        return kept.astype(jnp.bfloat16)

    def high_steps(kept):
        rows = model_width // copies
        places = list(range(1, copies.bit_length() - 1))
        half = kept.shape[1] // 2
        halves = []
        for part, order in ((kept[:, :half], places[::-1]), (kept[:, half:], places)):
            blocks = part.reshape(-1, rows, half)
            left = list(places)
            for place in order:
                low = 2 ** sum(p < place for p in left)
                left.remove(place)
                blocks = blocks.reshape(-1, 2, low, rows, half)
                mine = (copy >> place) & 1
                keep = lax.dynamic_index_in_dim(blocks, mine, 1, keepdims=False)
                give = lax.dynamic_index_in_dim(blocks, 1 - mine, 1, keepdims=False)
                come = flip(give, "dp", 1 << place)
                blocks = keep.astype(jnp.float32) + come.astype(jnp.float32)
                blocks = blocks.astype(jnp.bfloat16).reshape(-1, rows, half)
            halves.append(blocks[0])
        return jnp.concatenate(halves, axis=1)

    def scatter_copies(whole):
        return lax.psum_scatter(whole, "dp", scatter_dimension=0, tiled=True)

    def column_sums(array_in):
        return jnp.sum(array_in.astype(jnp.float32), axis=0)

    qkv_weight = by_pairs(query_weight, key_weight, value_weight)
    qkv_bias = by_pairs(query_bias, jnp.zeros_like(query_bias), value_bias)
    token_total = total(lengths, ("dp",))[0].astype(jnp.float32)
    grad_scale = seq_len * copies / (2.0 * token_total)
    first_part = own_part(jnp.concatenate([inner_weight, output_weight], axis=1))
    later_part = own_part(jnp.concatenate([outer_weight, qkv_weight], axis=1))
    first_parts = others(first_part)
    qkv = (matmul(hidden_in, qkv_weight) + qkv_bias).astype(jnp.bfloat16)
    contexts, extended, received = [], [], []
    for pair in range(pairs):
        context, queries = attend_forward(lengths, qkv, pair)
        contexts.append(context)
        extended.append(queries)
        blocks = spread(context)
        if pair == 0:
            first_parts, qkv, blocks, later_part = tie(first_parts, qkv, blocks, later_part)
            first_rows = gathered(first_parts)
            later_parts = others(later_part)
            blocks = [jnp.concatenate([b, inner_bias.reshape(-1, PAIR)]) for b in blocks]
        if pair == pairs - 1:
            later_parts, blocks = tie(later_parts, blocks)
            outer_rest = gathered(later_parts[..., :units])
            qkv_rest = gathered(later_parts[..., units:])
        received.append(exchange(blocks))
    inner_biases = [r[share_rows:].reshape(-1) for r in received[0]]
    received[0] = [r[:share_rows] for r in received[0]]
    context_all = jnp.concatenate(
        [received[p][s] for s in range(ranks) for p in range(pairs)], axis=1
    )
    inner_weights = [inner_weight] + [first_rows[s][:, :units] for s in range(ranks - 1)]
    output_weight_all = jnp.concatenate(
        [output_weight] + [first_rows[s][:, units:] for s in range(ranks - 1)], axis=1
    )
    outer_weights = [outer_weight] + [outer_rest[s] for s in range(ranks - 1)]
    qkv_weights = [qkv_weight] + [qkv_rest[s] for s in range(ranks - 1)]

    hidden_own = take_own(hidden_in).astype(jnp.float32)
    attention = times_rows(context_all, output_weight_all)
    normed, normal_one, inverse_one = layer_norm(
        hidden_own + (attention + output_bias), first_gain, first_shift
    )
    normed_low = normed.astype(jnp.bfloat16)
    activated, slopes = [], []
    branch = outer_bias.astype(jnp.float32)
    for s in range(ranks):
        value, slope = gelu_parts(matmul(normed_low, inner_weights[s]) + inner_biases[s])
        activated.append(value.astype(jnp.bfloat16))
        slopes.append(slope.astype(jnp.bfloat16))
        branch = branch + times_rows(activated[s], outer_weights[s])
    final, normal_two, inverse_two = layer_norm(normed + branch, second_gain, second_shift)
    row_mask = take_own(row_valid)[:, None]
    difference = final - take_own(teacher).astype(jnp.float32)
    loss_part = jnp.sum(jnp.where(row_mask, difference * difference, 0.0))
    final_grad = jnp.where(
        row_mask, take_own(cotangent).astype(jnp.float32) + grad_scale * difference, 0.0
    )
    second_grad = norm_back(final_grad, normal_two, inverse_two, second_gain)
    branch_low = second_grad.astype(jnp.bfloat16)
    activated_all = jnp.concatenate(activated, axis=1)
    outer_give = first_give(branch_low, activated_all)
    outer_give, branch_low = tie(outer_give, branch_low)
    outer_come = flip(outer_give, "dp", 1)
    inner_lows = []
    normed_grad = second_grad
    for s in range(ranks):
        inner_low = (matmul(branch_low, outer_weights[s]) * slopes[s]).astype(jnp.bfloat16)
        inner_lows.append(inner_low)
        if s == 0:
            outer_kept = first_keep(branch_low, activated_all, outer_come)
            inner_low, outer_kept = tie(inner_low, outer_kept)
        normed_grad = normed_grad + times_rows(inner_low, inner_weights[s])
    first_grad = norm_back(normed_grad, normal_one, inverse_one, first_gain)
    attention_low = first_grad.astype(jnp.bfloat16)
    grad_all = matmul(attention_low, output_weight_all).astype(jnp.bfloat16)
    grads = exchange(jnp.split(grad_all, ranks, axis=1))
    context_grad = jnp.zeros((seq_len, heads_width), jnp.bfloat16)
    for s in range(ranks):
        context_grad = lax.dynamic_update_slice_in_dim(
            context_grad, grads[s], (rank ^ s) * share_rows, 0
        )
    inner_low_all = jnp.concatenate(inner_lows, axis=1)
    inner_whole = over_rows(normed_low, inner_low_all).astype(jnp.bfloat16)
    output_whole = over_rows(attention_low, context_all).astype(jnp.bfloat16)
    outer_rows = high_steps(outer_kept)
    context_grad, inner_whole, output_whole = tie(context_grad, inner_whole, output_whole)
    inner_rows = scatter_copies(inner_whole)

    input_rows = first_grad
    query_sums = []
    for pair in range(pairs):
        qkv_low = attend_backward(lengths, extended[pair], qkv, contexts[pair], context_grad, pair)
        blocks = spread(qkv_low)
        qkv_whole = over_rows(hidden_in, qkv_low).astype(jnp.bfloat16)
        if pair == 0:
            blocks, context_grad, outer_rows, qkv_whole = tie(
                blocks, context_grad, outer_rows, qkv_whole
            )
            both = scatter_copies(jnp.concatenate([output_whole, qkv_whole], axis=1))
            output_rows, qkv_sums = both[:, :model_width], [both[:, model_width:]]
            outer_weight_grad = reduce_ranks(jnp.split(outer_rows, ranks, axis=1))
        else:
            blocks, qkv_low = tie(blocks, qkv_low)
            come = flip(first_give(hidden_in, qkv_low), "dp", 1)
            qkv_sums.append(high_steps(first_keep(hidden_in, qkv_low, come)))
        columns = slice(3 * PAIR * pair, 3 * PAIR * (pair + 1))
        for block, weight in zip(exchange(blocks), qkv_weights):
            input_rows = input_rows + times_rows(block, weight[:, columns])
        query_sums.append(column_sums(qkv_low[:, :PAIR]))
    inner_parts = jnp.split(inner_rows, ranks, axis=1)
    output_parts = jnp.split(output_rows, ranks, axis=1)
    both_sum = reduce_ranks(
        [jnp.concatenate([i, o], axis=1) for i, o in zip(inner_parts, output_parts)]
    )
    inner_weight_grad, output_weight_grad = both_sum[:, :units], both_sum[:, units:]
    qkv_sums = [jnp.split(w.astype(jnp.float32), 3, axis=1) for w in qkv_sums]
    query_weight_grad, key_weight_grad, value_weight_grad = [
        jnp.concatenate([w[i] for w in qkv_sums], axis=1) for i in range(3)
    ]

    query_sums = lax.dynamic_update_slice_in_dim(
        jnp.zeros((model_width,), jnp.float32), jnp.concatenate(query_sums), rank * heads_width, 0
    )
    vectors = [
        ordered(column_sums(inner_low_all)),
        column_sums(attention_low),
        column_sums(normed_grad * normal_one),
        column_sums(normed_grad),
        column_sums(branch_low),
        column_sums(final_grad * normal_two),
        column_sums(final_grad),
        ordered(column_sums(grad_all)),
        query_sums,
        jnp.full((model_width,), loss_part),
    ]
    vectors = total(jnp.concatenate(vectors).reshape(-1, model_width), ("dp", "tensor"))
    wide = ranks * units // model_width
    inner_bias_grad = vectors[:wide].reshape(-1)
    (
        output_bias_grad,
        first_gain_grad,
        first_shift_grad,
        outer_bias_grad,
        second_gain_grad,
        second_shift_grad,
        value_bias_grad,
        query_bias_grad,
    ) = [vectors[wide + i] for i in range(8)]
    return (
        final.astype(jnp.bfloat16),
        vectors[wide + 8, 0] / token_total,
        input_rows,
        query_weight_grad,
        query_bias_grad,
        key_weight_grad,
        value_weight_grad,
        value_bias_grad,
        output_weight_grad,
        output_bias_grad,
        first_gain_grad,
        first_shift_grad,
        inner_weight_grad,
        inner_bias_grad,
        outer_weight_grad,
        outer_bias_grad,
        second_gain_grad,
        second_shift_grad,
    )


def solution(mesh):
    rows, columns, split = P("dp", None), P(None, "tensor"), P("dp", "tensor")
    part, whole, own = P("tensor"), P(), P(("dp", "tensor"), None)
    in_specs = (
        rows,
        P("dp"),
        columns,
        part,
        columns,
        columns,
        part,
        columns,
        whole,
        whole,
        whole,
        columns,
        part,
        columns,
        whole,
        whole,
        whole,
        rows,
        rows,
    )
    out_specs = (
        own,
        whole,
        own,
        split,
        whole,
        split,
        split,
        whole,
        split,
        whole,
        whole,
        whole,
        split,
        whole,
        split,
        whole,
        whole,
        whole,
    )
    return jax.shard_map(shards, mesh=mesh, in_specs=in_specs, out_specs=out_specs, check_vma=False)
```

```python
import jax
import jax.numpy as jnp
from jax import lax
from jax.experimental import pallas as pl
from jax.experimental.pallas import tpu as pltpu
from jax.sharding import PartitionSpec as P

HD = 64
PAIR = 128
VMEM_BYTES = 60000 * 1024


epsilon = 1e-05


def matmul(former, latter):
    return jnp.dot(former, latter, preferred_element_type=jnp.float32)


def times_rows(former, latter):
    return lax.dot_general(
        former, latter, (((1,), (1,)), ((), ())), preferred_element_type=jnp.float32
    )


def over_rows(former, latter):
    return lax.dot_general(
        former, latter, (((0,), (0,)), ((), ())), preferred_element_type=jnp.float32
    )


def layer_norm(hidden, norm_gain, norm_shift):
    centered = hidden - jnp.mean(hidden, axis=-1, keepdims=True)
    inverse = lax.rsqrt(jnp.mean(centered * centered, axis=-1, keepdims=True) + epsilon)
    normal = centered * inverse
    return (normal * norm_gain + norm_shift, normal, inverse)


def norm_back(upstream, normal, inverse, norm_gain):
    scaled = upstream * norm_gain
    return inverse * (
        scaled
        - jnp.mean(scaled, axis=-1, keepdims=True)
        - normal * jnp.mean(scaled * normal, axis=-1, keepdims=True)
    )


def gelu_parts(values):
    cumulative = 0.5 * (1.0 + jax.scipy.special.erf(values * 0.7071067811865476))
    slope = cumulative + values * jnp.exp(-0.5 * values * values) * 0.3989422804014327
    return (values * cumulative, slope)


def lanes(rows):
    return lax.broadcasted_iota(jnp.int32, (rows, PAIR), 1)


def in_head(lane, head):
    return (lane < HD) if head == 0 else (lane >= HD)


def extend(base, lane, head, first, offset):
    start = HD * (1 - head)
    high = offset.astype(jnp.bfloat16).astype(jnp.float32)
    middle = (offset - high).astype(jnp.bfloat16).astype(jnp.float32)
    out = jnp.where(lane == start, first, 0.0)
    out = jnp.where(lane == start + 1, -high, out)
    out = jnp.where(lane == start + 2, -middle, out)
    out = jnp.where(lane == start + 3, high + middle - offset, out)
    return jnp.where(in_head(lane, head), base, out).astype(jnp.bfloat16)


def extend_keys(keys, lane, head, row_start, length):
    start = HD * (1 - head)
    position = row_start + lax.broadcasted_iota(jnp.int32, keys.shape, 0)
    bias = jnp.where(position < length, 0.0, -1e30)
    ones = jnp.where((lane > start) & (lane < start + 4), 1.0, 0.0)
    side = jnp.where(lane == start, bias, ones)
    return jnp.where(in_head(lane, head), keys, side).astype(jnp.bfloat16)


def extend_values(values, lane, head):
    return jnp.where(in_head(lane, head), values, 1.0).astype(jnp.bfloat16)


def forward_kernel(length_ref, q_ref, k_ref, v_ref, context_ref, extended_ref, keys, values):
    @pl.when(pl.program_id(0) == 0)
    def _():
        lane = lanes(k_ref.shape[0])
        k_float = k_ref[...].astype(jnp.float32)
        v_float = v_ref[...].astype(jnp.float32)
        for head in range(2):
            keys[head] = extend_keys(k_float, lane, head, 0, length_ref[0])
            values[head] = extend_values(v_float, lane, head)

    lane = lanes(q_ref.shape[0])
    scaled = q_ref[...].astype(jnp.float32) * HD**-0.5
    contexts = []
    for head in range(2):
        plain = jnp.where(lane == HD * (1 - head), 1.0, 0.0)
        query = jnp.where(in_head(lane, head), scaled, plain).astype(jnp.bfloat16)
        scores = times_rows(query, keys[head])
        peak = jnp.max(scores, axis=1, keepdims=True)
        exponent = jnp.exp(scores - peak).astype(jnp.bfloat16)
        out = matmul(exponent, values[head])
        contexts.append(out / pltpu.roll(out, HD, 1))
        extended_ref[head] = extend(scaled, lane, head, 1.0, peak + jnp.log(out))
    context_ref[...] = jnp.where(lane < HD, contexts[0], contexts[1]).astype(jnp.bfloat16)


def attend_forward(length, qkv, pair):
    seq_len = qkv.shape[0]
    rows = min(256, seq_len)
    return pl.pallas_call(
        forward_kernel,
        grid_spec=pltpu.PrefetchScalarGridSpec(
            num_scalar_prefetch=1,
            grid=(seq_len // rows,),
            in_specs=[
                pl.BlockSpec((rows, PAIR), lambda i, n: (i, 3 * pair)),
                pl.BlockSpec((seq_len, PAIR), lambda i, n: (0, 3 * pair + 1)),
                pl.BlockSpec((seq_len, PAIR), lambda i, n: (0, 3 * pair + 2)),
            ],
            out_specs=[
                pl.BlockSpec((rows, PAIR), lambda i, n: (i, 0)),
                pl.BlockSpec((2, rows, PAIR), lambda i, n: (0, i, 0)),
            ],
            scratch_shapes=[pltpu.VMEM((2, seq_len, PAIR), jnp.bfloat16)] * 2,
        ),
        out_shape=[
            jax.ShapeDtypeStruct((seq_len, PAIR), jnp.bfloat16),
            jax.ShapeDtypeStruct((2, seq_len, PAIR), jnp.bfloat16),
        ],
        compiler_params=pltpu.CompilerParams(vmem_limit_bytes=VMEM_BYTES),
        cost_estimate=pl.CostEstimate(
            flops=8 * seq_len * seq_len * 2 * PAIR,
            bytes_accessed=12 * seq_len * PAIR,
            transcendentals=2 * seq_len * seq_len,
        ),
        name="attend_forward",
    )(length, qkv, qkv, qkv)


def backward_kernel(length_ref, extended_ref, k_ref, v_ref, context_ref, grad_ref, out_ref, grads, turned):
    step = pl.program_id(0)
    seq_len, rows = grad_ref.shape[0], k_ref.shape[0]

    @pl.when(step == 0)
    def _():
        def prepare(j, carry):
            here = pl.ds(pl.multiple_of(j * rows, rows), rows)
            lane = lanes(rows)
            grad = grad_ref[here, :].astype(jnp.float32)
            product = grad * context_ref[here, :].astype(jnp.float32)
            for head in range(2):
                centre = jnp.sum(
                    jnp.where(in_head(lane, head), product, 0.0), axis=1, keepdims=True
                )
                grads[head, here, :] = extend(grad, lane, head, 0.0, centre)
            return carry

        lax.fori_loop(0, seq_len // rows, prepare, 0)

    lane = lanes(rows)
    k_float = k_ref[...].astype(jnp.float32)
    v_float = v_ref[...].astype(jnp.float32)
    across = k_float.T.astype(jnp.bfloat16)
    key_grads, value_grads = [], []
    for head in range(2):
        keys = extend_keys(k_float, lane, head, step * rows, length_ref[0])
        values = extend_values(v_float, lane, head)
        query, grad = extended_ref[head], grads[head]
        probs = jnp.exp(times_rows(keys, query))
        score_grad = (probs * times_rows(values, grad)).astype(jnp.bfloat16)
        value_grads.append(matmul(probs.astype(jnp.bfloat16), grad))
        key_grads.append(matmul(score_grad, query))
        own = slice(HD * head, HD * (head + 1))
        part = matmul(across[own], score_grad)

        @pl.when(step == 0)
        def _():
            turned[own, :] = part

        @pl.when(step > 0)
        def _():
            turned[own, :] += part

    here = pl.ds(pl.multiple_of(step * rows, rows), rows)
    key_grad = jnp.where(lane < HD, key_grads[0], key_grads[1])
    value_grad = jnp.where(lane < HD, value_grads[0], value_grads[1])
    out_ref[here, PAIR : 2 * PAIR] = key_grad.astype(jnp.bfloat16)
    out_ref[here, 2 * PAIR :] = value_grad.astype(jnp.bfloat16)

    @pl.when(step == pl.num_programs(0) - 1)
    def _():
        def finish(j, carry):
            here = pl.ds(pl.multiple_of(j * rows, rows), rows)
            out_ref[here, :PAIR] = (turned[:, here].T * HD**-0.5).astype(jnp.bfloat16)
            return carry

        lax.fori_loop(0, seq_len // rows, finish, 0)


def attend_backward(length, extended, qkv, context, context_grad, pair):
    seq_len = qkv.shape[0]
    rows = min(256, seq_len)
    return pl.pallas_call(
        backward_kernel,
        grid_spec=pltpu.PrefetchScalarGridSpec(
            num_scalar_prefetch=1,
            grid=(seq_len // rows,),
            in_specs=[
                pl.BlockSpec((2, seq_len, PAIR), lambda i, n: (0, 0, 0)),
                pl.BlockSpec((rows, PAIR), lambda i, n: (i, 3 * pair + 1)),
                pl.BlockSpec((rows, PAIR), lambda i, n: (i, 3 * pair + 2)),
                pl.BlockSpec((seq_len, PAIR), lambda i, n: (0, 0)),
                pl.BlockSpec((seq_len, PAIR), lambda i, n: (0, pair)),
            ],
            out_specs=pl.BlockSpec((seq_len, 3 * PAIR), lambda i, n: (0, 0)),
            scratch_shapes=[
                pltpu.VMEM((2, seq_len, PAIR), jnp.bfloat16),
                pltpu.VMEM((PAIR, seq_len), jnp.float32),
            ],
        ),
        out_shape=jax.ShapeDtypeStruct((seq_len, 3 * PAIR), jnp.bfloat16),
        compiler_params=pltpu.CompilerParams(vmem_limit_bytes=VMEM_BYTES),
        cost_estimate=pl.CostEstimate(
            flops=20 * seq_len * seq_len * 2 * PAIR,
            bytes_accessed=20 * seq_len * PAIR,
            transcendentals=2 * seq_len * seq_len,
        ),
        name="attend_backward",
    )(length, extended, qkv, qkv, context, context_grad)


def tie(*values):
    return lax.optimization_barrier(values)


def flip(array_in, axis_name, bits):
    size = lax.axis_size(axis_name)
    return lax.ppermute(array_in, axis_name, [(i, i ^ bits) for i in range(size)])


def total(array_in, axis_names):
    for name in axis_names:
        bits = 1
        while bits < lax.axis_size(name):
            array_in = array_in + flip(array_in, name, bits)
            bits *= 2
    return array_in


def shards(
    hidden_in,
    lengths,
    query_weight,
    query_bias,
    key_weight,
    value_weight,
    value_bias,
    output_weight,
    output_bias,
    first_gain,
    first_shift,
    inner_weight,
    inner_bias,
    outer_weight,
    outer_bias,
    second_gain,
    second_shift,
    cotangent,
    teacher,
):
    seq_len, model_width = hidden_in.shape
    ranks = lax.axis_size("tensor")
    rank = lax.axis_index("tensor")
    copies = lax.axis_size("dp")
    copy = lax.axis_index("dp")
    share_rows = seq_len // ranks
    heads_width = query_weight.shape[1]
    units = inner_weight.shape[1]
    pairs = heads_width // PAIR
    row_valid = jnp.arange(seq_len, dtype=jnp.int32) < lengths[0]

    def take_own(array_in):
        return lax.dynamic_slice_in_dim(array_in, rank * share_rows, share_rows, 0)

    def by_pairs(*arrays):
        return jnp.concatenate(
            [a[..., p * PAIR : (p + 1) * PAIR] for p in range(pairs) for a in arrays], axis=-1
        )

    def own_part(weight):
        rows = weight.shape[0] // copies
        return lax.dynamic_slice_in_dim(weight, copy * rows, rows, 0)

    def others(part):
        return jnp.stack([flip(part, "tensor", s) for s in range(1, ranks)])

    def gathered(parts):
        return lax.all_gather(parts, "dp", axis=1, tiled=True)

    def trade(blocks):
        return lax.all_to_all(blocks, "tensor", 0, 0)

    def block_of(blocks, s):
        return lax.dynamic_index_in_dim(blocks, rank ^ s, 0, keepdims=False)

    def reordered(blocks):
        return jnp.stack([block_of(blocks, s) for s in range(ranks)])

    def column_blocks(array_in):
        width = array_in.shape[1] // ranks
        return jnp.stack(
            [
                lax.dynamic_slice_in_dim(array_in, (rank ^ i) * width, width, 1)
                for i in range(ranks)
            ]
        )

    def add_blocks(blocks):
        return sum(blocks[i].astype(jnp.float32) for i in range(ranks))

    def ordered(vector_in):
        table = vector_in.reshape(ranks, -1)
        return jnp.concatenate(
            [lax.dynamic_index_in_dim(table, rank ^ s, 0, keepdims=False) for s in range(ranks)]
        )

    def half_columns(array_in, other):
        blocks = jnp.split(array_in, copies, axis=1)
        odd = ((copy & 1) ^ other) == 1
        return jnp.concatenate(
            [jnp.where(odd, blocks[i + 1], blocks[i]) for i in range(0, copies, 2)], axis=1
        )

    def half_rows(whole, other):
        blocks = whole.reshape(copies // 2, 2, -1, whole.shape[1])
        return lax.dynamic_index_in_dim(blocks, (copy & 1) ^ other, 1, keepdims=False)

    def halves_of(kept):
        places = list(range(1, copies.bit_length() - 1))
        middle = len(kept) // 2
        states = []
        for part, order in ((kept[:middle], places[::-1]), (kept[middle:], places)):
            blocks = jnp.stack([k.reshape(copies // 2, -1, k.shape[-1]) for k in part], axis=1)
            states.append((blocks, list(places), order))
        return states

    def begin(states):
        started = []
        for blocks, left, order in states:
            place = order[0]
            low = 2 ** sum(p < place for p in left)
            split = blocks.reshape(-1, 2, low, *blocks.shape[1:])
            mine = (copy >> place) & 1
            keep = lax.dynamic_index_in_dim(split, mine, 1, keepdims=False)
            give = lax.dynamic_index_in_dim(split, 1 - mine, 1, keepdims=False)
            started.append((keep, flip(give, "dp", 1 << place)))
        return started

    def complete(states, started):
        out = []
        for (blocks, left, order), (keep, come) in zip(states, started):
            added = keep.astype(jnp.float32) + come.astype(jnp.float32)
            added = added.astype(jnp.bfloat16).reshape(-1, *blocks.shape[1:])
            out.append((added, [p for p in left if p != order[0]], order[1:]))
        return out

    def step(states):
        return complete(states, begin(states))

    def finished(states):
        while states[0][2]:
            states = step(states)
        return [part for blocks, _, _ in states for part in blocks[0]]

    def scatter_copies(whole):
        return lax.psum_scatter(whole, "dp", scatter_dimension=0, tiled=True)

    def column_sums(array_in):
        return jnp.sum(array_in.astype(jnp.float32), axis=0)

    qkv_weight = by_pairs(query_weight, key_weight, value_weight)
    qkv_bias = by_pairs(query_bias, jnp.zeros_like(query_bias), value_bias)
    output_part, both_part = own_part(output_weight), own_part(
        jnp.concatenate([inner_weight, outer_weight], axis=1)
    )
    part_rows = output_part.shape[0]
    bias_rows = inner_bias.reshape(-1, heads_width)
    output_part = jnp.concatenate([output_part, bias_rows, jnp.zeros_like(bias_rows)])
    output_parts = trade(jnp.broadcast_to(output_part, (ranks, *output_part.shape)))
    near_part = flip(both_part, "tensor", 1)
    qkv_part = own_part(qkv_weight)
    qkv = (matmul(hidden_in, qkv_weight) + qkv_bias).astype(jnp.bfloat16)
    output_parts, near_part, qkv, both_part = tie(output_parts, near_part, qkv, both_part)
    far_parts = [flip(both_part, "tensor", s) for s in range(2, ranks)]
    output_others = [block_of(output_parts, s) for s in range(1, ranks)]
    output_rest = [p[:part_rows] for p in output_others]
    biases = [p[part_rows : part_rows + bias_rows.shape[0]] for p in output_others]

    column = lax.broadcasted_iota(jnp.int32, (part_rows, PAIR), 1)
    digits = jnp.where(column == 0, lengths[0] // 256, lengths[0] % 256).astype(jnp.bfloat16)
    near_rows = lax.all_gather(
        jnp.concatenate([near_part, *output_rest, digits], axis=1), "dp", axis=0, tiled=True
    )
    contexts, extended = [], []
    for pair in range(pairs):
        context, queries = attend_forward(lengths, qkv, pair)
        contexts.append(context)
        extended.append(queries)
    far_parts, contexts = tie(far_parts, contexts)
    far_rows = gathered(jnp.stack(far_parts))
    received = trade(jnp.concatenate(contexts, axis=1).reshape(ranks, share_rows, -1))
    digits = near_rows[::part_rows, -PAIR:].astype(jnp.float32)
    token_total = jnp.sum(256.0 * digits[:, 0] + digits[:, 1])
    grad_scale = seq_len * copies / (2.0 * token_total)
    context_all = jnp.concatenate(
        [block_of(received, s) for s in range(ranks)], axis=1
    )
    both_rest = [near_rows[:, : 2 * units]] + [far_rows[i] for i in range(ranks - 2)]
    inner_weights = [inner_weight] + [rest[:, :units] for rest in both_rest]
    outer_weights = [outer_weight] + [rest[:, units:] for rest in both_rest]
    inner_biases = [inner_bias] + [b.reshape(-1) for b in biases]
    output_weight_all = jnp.concatenate([output_weight, near_rows[:, 2 * units : -PAIR]], axis=1)

    hidden_own = take_own(hidden_in).astype(jnp.float32)
    attention = times_rows(context_all, output_weight_all)
    normed, normal_one, inverse_one = layer_norm(
        hidden_own + (attention + output_bias), first_gain, first_shift
    )
    normed_low = normed.astype(jnp.bfloat16)
    activated, slopes = [], []
    branch = outer_bias.astype(jnp.float32)
    for s in range(ranks):
        value, slope = gelu_parts(matmul(normed_low, inner_weights[s]) + inner_biases[s])
        activated.append(value.astype(jnp.bfloat16))
        slopes.append(slope.astype(jnp.bfloat16))
        branch = branch + times_rows(activated[s], outer_weights[s])
    final, normal_two, inverse_two = layer_norm(normed + branch, second_gain, second_shift)
    row_mask = take_own(row_valid)[:, None]
    difference = final - take_own(teacher).astype(jnp.float32)
    loss_part = jnp.sum(jnp.where(row_mask, difference * difference, 0.0))
    final_grad = jnp.where(
        row_mask, take_own(cotangent).astype(jnp.float32) + grad_scale * difference, 0.0
    )
    second_grad = norm_back(final_grad, normal_two, inverse_two, second_gain)
    branch_low = second_grad.astype(jnp.bfloat16)
    outer_whole = over_rows(branch_low, jnp.concatenate(activated, axis=1)).astype(jnp.bfloat16)
    outer_whole, branch_low, qkv_part = tie(outer_whole, branch_low, qkv_part)
    outer_rows = scatter_copies(outer_whole)
    qkv_parts = trade(jnp.broadcast_to(qkv_part, (ranks, *qkv_part.shape)))
    qkv_rest = gathered(jnp.stack([block_of(qkv_parts, s) for s in range(1, ranks)]))
    qkv_weights = [qkv_weight] + [qkv_rest[s] for s in range(ranks - 1)]
    inner_lows = []
    normed_grad = second_grad
    for s in range(ranks):
        inner_low = (matmul(branch_low, outer_weights[s]) * slopes[s]).astype(jnp.bfloat16)
        inner_lows.append(inner_low)
        normed_grad = normed_grad + times_rows(inner_low, inner_weights[s])
    first_grad = norm_back(normed_grad, normal_one, inverse_one, first_gain)
    attention_low = first_grad.astype(jnp.bfloat16)
    grad_all = matmul(attention_low, output_weight_all).astype(jnp.bfloat16)
    grad_all, inner_lows = tie(grad_all, inner_lows)
    context_grad = trade(column_blocks(grad_all)).reshape(seq_len, heads_width)
    give_columns, keep_columns = half_columns(normed_low, 1), half_columns(normed_low, 0)
    inner_kept = []
    for s in range(ranks):
        give = over_rows(give_columns, inner_lows[s]).astype(jnp.bfloat16)
        come = flip(give, "dp", 1).astype(jnp.float32)
        kept = over_rows(keep_columns, inner_lows[s]) + come
        inner_kept.append(kept.astype(jnp.bfloat16))
    output_whole = over_rows(attention_low, context_all).astype(jnp.bfloat16)
    inner_states = halves_of(inner_kept)
    inner_started = begin(inner_states)
    vectors = [
        ordered(jnp.concatenate([column_sums(low) for low in inner_lows])),
        column_sums(attention_low),
        column_sums(normed_grad * normal_one),
        column_sums(normed_grad),
        column_sums(branch_low),
        column_sums(final_grad * normal_two),
        column_sums(final_grad),
        ordered(column_sums(grad_all)),
        jnp.full((model_width,), loss_part),
    ]
    vectors = jnp.concatenate(vectors).reshape(-1, model_width)
    vectors = vectors + flip(vectors, "dp", 1)
    context_grad, inner_kept, output_whole, vectors = tie(
        context_grad, inner_kept, output_whole, vectors
    )
    outer_come = trade(column_blocks(outer_rows))
    bits = [1 << p for p in range(1, copies.bit_length() - 1)]
    vector_come = flip(vectors, "dp", bits[0])

    def add_input(rows, moved, columns):
        for s, weight in enumerate(qkv_weights):
            rows = rows + times_rows(block_of(moved, s), weight[:, columns])
        return rows

    input_rows = first_grad
    query_sums = []
    for pair in range(pairs):
        qkv_low = attend_backward(lengths, extended[pair], qkv, contexts[pair], context_grad, pair)
        if pair == 0:
            qkv_low, inner_started, outer_come, vector_come = tie(
                qkv_low, inner_started, outer_come, vector_come
            )
            outer_weight_grad = add_blocks(outer_come)
            inner_states = complete(inner_states, inner_started)
            inner_started = begin(inner_states) if inner_states[0][2] else None
            vectors = vectors + vector_come
            vector_come = flip(vectors, "dp", bits[1])
        if pair == 0:
            qkv_whole = over_rows(hidden_in, qkv_low).astype(jnp.bfloat16)
            both = jnp.concatenate([output_whole, qkv_whole], axis=1)
            context_grad, both = tie(context_grad, both)
            both = scatter_copies(both)
            output_rows, qkv_sums = both[:, :model_width], [both[:, model_width:]]
        else:
            moved, qkv_low, inner_started, vector_come = tie(
                moved, qkv_low, inner_started, vector_come
            )
            vectors = vectors + vector_come
        columns = slice(3 * PAIR * pair, 3 * PAIR * (pair + 1))
        if pair > 0:
            input_rows = add_input(input_rows, moved, last_columns)
        moved, last_columns = trade(qkv_low.reshape(ranks, share_rows, -1)), columns
        if pair > 0:
            qkv_whole = over_rows(hidden_in, qkv_low).astype(jnp.bfloat16)
            come = flip(half_rows(qkv_whole, 1), "dp", 1).astype(jnp.float32)
            kept = (half_rows(qkv_whole, 0).astype(jnp.float32) + come).astype(jnp.bfloat16)
            kept = kept.reshape(-1, kept.shape[-1])
            pieces = finished(halves_of(jnp.split(kept, 2, axis=1)))
            qkv_sums.append(jnp.concatenate(pieces, axis=1))
        query_sums.append(column_sums(qkv_low[:, :PAIR]))
    inner_states = complete(inner_states, inner_started)
    inner_parts = finished(inner_states)
    output_parts = jnp.split(output_rows, ranks, axis=1)
    last = jnp.stack([jnp.concatenate([i, o], axis=1) for i, o in zip(inner_parts, output_parts)])
    moved, last = tie(moved, reordered(last))
    input_rows = add_input(input_rows, moved, last_columns)
    both_sum = add_blocks(trade(last))
    inner_weight_grad, output_weight_grad = both_sum[:, :units], both_sum[:, units:]
    qkv_sums = [jnp.split(w.astype(jnp.float32), 3, axis=1) for w in qkv_sums]
    query_weight_grad, key_weight_grad, value_weight_grad = [
        jnp.concatenate([w[i] for w in qkv_sums], axis=1) for i in range(3)
    ]

    if pairs == 1:
        vectors = vectors + vector_come
    for bit in bits[2:]:
        vectors = vectors + flip(vectors, "dp", bit)
    query_sums = total(jnp.concatenate(query_sums).reshape(-1, PAIR), ("dp",)).reshape(-1)
    query_sums = lax.dynamic_update_slice_in_dim(
        jnp.zeros((model_width,), jnp.float32), query_sums, rank * heads_width, 0
    )
    vectors = total(jnp.concatenate([vectors, query_sums[None]]), ("tensor",))
    wide = ranks * units // model_width
    inner_bias_grad = vectors[:wide].reshape(-1)
    (
        output_bias_grad,
        first_gain_grad,
        first_shift_grad,
        outer_bias_grad,
        second_gain_grad,
        second_shift_grad,
        value_bias_grad,
    ) = [vectors[wide + i] for i in range(7)]
    query_bias_grad = vectors[wide + 8]
    return (
        final.astype(jnp.bfloat16),
        vectors[wide + 7, 0] / token_total,
        input_rows,
        query_weight_grad,
        query_bias_grad,
        key_weight_grad,
        value_weight_grad,
        value_bias_grad,
        output_weight_grad,
        output_bias_grad,
        first_gain_grad,
        first_shift_grad,
        inner_weight_grad,
        inner_bias_grad,
        outer_weight_grad,
        outer_bias_grad,
        second_gain_grad,
        second_shift_grad,
    )


def solution(mesh):
    rows, columns, split = P("dp", None), P(None, "tensor"), P("dp", "tensor")
    part, whole, own = P("tensor"), P(), P(("dp", "tensor"), None)
    in_specs = (
        rows,
        P("dp"),
        columns,
        part,
        columns,
        columns,
        part,
        columns,
        whole,
        whole,
        whole,
        columns,
        part,
        columns,
        whole,
        whole,
        whole,
        rows,
        rows,
    )
    out_specs = (
        own,
        whole,
        own,
        split,
        whole,
        split,
        split,
        whole,
        split,
        whole,
        whole,
        whole,
        split,
        whole,
        split,
        whole,
        whole,
        whole,
    )
    return jax.shard_map(shards, mesh=mesh, in_specs=in_specs, out_specs=out_specs, check_vma=False)
```

```python
import jax
import jax.numpy as jnp
from jax import lax
from jax.experimental import pallas as pl
from jax.experimental.pallas import tpu as pltpu
from jax.sharding import PartitionSpec as P

HD = 64
PAIR = 128
VMEM_BYTES = 60000 * 1024


epsilon = 1e-05


def matmul(former, latter):
    return jnp.dot(former, latter, preferred_element_type=jnp.float32)


def times_rows(former, latter):
    return lax.dot_general(
        former, latter, (((1,), (1,)), ((), ())), preferred_element_type=jnp.float32
    )


def over_rows(former, latter):
    return lax.dot_general(
        former, latter, (((0,), (0,)), ((), ())), preferred_element_type=jnp.float32
    )


def layer_norm(hidden, norm_gain, norm_shift):
    centered = hidden - jnp.mean(hidden, axis=-1, keepdims=True)
    inverse = lax.rsqrt(jnp.mean(centered * centered, axis=-1, keepdims=True) + epsilon)
    normal = centered * inverse
    return (normal * norm_gain + norm_shift, normal, inverse)


def norm_back(upstream, normal, inverse, norm_gain):
    scaled = upstream * norm_gain
    return inverse * (
        scaled
        - jnp.mean(scaled, axis=-1, keepdims=True)
        - normal * jnp.mean(scaled * normal, axis=-1, keepdims=True)
    )


def gelu_parts(values):
    cumulative = 0.5 * (1.0 + jax.scipy.special.erf(values * 0.7071067811865476))
    slope = cumulative + values * jnp.exp(-0.5 * values * values) * 0.3989422804014327
    return (values * cumulative, slope)


def lanes(rows):
    return lax.broadcasted_iota(jnp.int32, (rows, PAIR), 1)


def in_head(lane, head):
    return (lane < HD) if head == 0 else (lane >= HD)


def extend(base, lane, head, first, offset):
    start = HD * (1 - head)
    high = offset.astype(jnp.bfloat16).astype(jnp.float32)
    middle = (offset - high).astype(jnp.bfloat16).astype(jnp.float32)
    out = jnp.where(lane == start, first, 0.0)
    out = jnp.where(lane == start + 1, -high, out)
    out = jnp.where(lane == start + 2, -middle, out)
    out = jnp.where(lane == start + 3, high + middle - offset, out)
    return jnp.where(in_head(lane, head), base, out).astype(jnp.bfloat16)


def extend_keys(keys, lane, head, row_start, length):
    start = HD * (1 - head)
    position = row_start + lax.broadcasted_iota(jnp.int32, keys.shape, 0)
    bias = jnp.where(position < length, 0.0, -1e30)
    ones = jnp.where((lane > start) & (lane < start + 4), 1.0, 0.0)
    side = jnp.where(lane == start, bias, ones)
    return jnp.where(in_head(lane, head), keys, side).astype(jnp.bfloat16)


def extend_values(values, lane, head):
    return jnp.where(in_head(lane, head), values, 1.0).astype(jnp.bfloat16)


def forward_kernel(length_ref, q_ref, k_ref, v_ref, context_ref, extended_ref, keys, values):
    @pl.when(pl.program_id(1) == 0)
    def _():
        lane = lanes(k_ref.shape[0])
        k_float = k_ref[...].astype(jnp.float32)
        v_float = v_ref[...].astype(jnp.float32)
        for head in range(2):
            keys[head] = extend_keys(k_float, lane, head, 0, length_ref[0])
            values[head] = extend_values(v_float, lane, head)

    lane = lanes(q_ref.shape[0])
    scaled = q_ref[...].astype(jnp.float32) * HD**-0.5
    contexts = []
    for head in range(2):
        plain = jnp.where(lane == HD * (1 - head), 1.0, 0.0)
        query = jnp.where(in_head(lane, head), scaled, plain).astype(jnp.bfloat16)
        scores = times_rows(query, keys[head])
        peak = jnp.max(scores, axis=1, keepdims=True)
        exponent = jnp.exp(scores - peak).astype(jnp.bfloat16)
        out = matmul(exponent, values[head])
        contexts.append(out / pltpu.roll(out, HD, 1))
        extended_ref[head] = extend(scaled, lane, head, 1.0, peak + jnp.log(out))
    context_ref[...] = jnp.where(lane < HD, contexts[0], contexts[1]).astype(jnp.bfloat16)


def attend_forward(length, qkv):
    seq_len = qkv.shape[0]
    pairs = qkv.shape[1] // (3 * PAIR)
    rows = min(256, seq_len)
    return pl.pallas_call(
        forward_kernel,
        grid_spec=pltpu.PrefetchScalarGridSpec(
            num_scalar_prefetch=1,
            grid=(pairs, seq_len // rows),
            in_specs=[
                pl.BlockSpec((rows, PAIR), lambda p, i, n: (i, 3 * p)),
                pl.BlockSpec((seq_len, PAIR), lambda p, i, n: (0, 3 * p + 1)),
                pl.BlockSpec((seq_len, PAIR), lambda p, i, n: (0, 3 * p + 2)),
            ],
            out_specs=[
                pl.BlockSpec((rows, PAIR), lambda p, i, n: (i, p)),
                pl.BlockSpec((2, rows, PAIR), lambda p, i, n: (p, i, 0)),
            ],
            scratch_shapes=[pltpu.VMEM((2, seq_len, PAIR), jnp.bfloat16)] * 2,
        ),
        out_shape=[
            jax.ShapeDtypeStruct((seq_len, pairs * PAIR), jnp.bfloat16),
            jax.ShapeDtypeStruct((2 * pairs, seq_len, PAIR), jnp.bfloat16),
        ],
        compiler_params=pltpu.CompilerParams(vmem_limit_bytes=VMEM_BYTES),
        cost_estimate=pl.CostEstimate(
            flops=8 * seq_len * seq_len * 2 * PAIR * pairs,
            bytes_accessed=12 * seq_len * PAIR * pairs,
            transcendentals=2 * seq_len * seq_len * pairs,
        ),
        name="attend_forward",
    )(length, qkv, qkv, qkv)


def backward_kernel(length_ref, extended_ref, k_ref, v_ref, context_ref, grad_ref, out_ref, grads, turned):
    step = pl.program_id(0)
    seq_len, rows = grad_ref.shape[0], k_ref.shape[0]

    @pl.when(step == 0)
    def _():
        def prepare(j, carry):
            here = pl.ds(pl.multiple_of(j * rows, rows), rows)
            lane = lanes(rows)
            grad = grad_ref[here, :].astype(jnp.float32)
            product = grad * context_ref[here, :].astype(jnp.float32)
            for head in range(2):
                centre = jnp.sum(
                    jnp.where(in_head(lane, head), product, 0.0), axis=1, keepdims=True
                )
                grads[head, here, :] = extend(grad, lane, head, 0.0, centre)
            return carry

        lax.fori_loop(0, seq_len // rows, prepare, 0)

    lane = lanes(rows)
    k_float = k_ref[...].astype(jnp.float32)
    v_float = v_ref[...].astype(jnp.float32)
    across = k_float.T.astype(jnp.bfloat16)
    key_grads, value_grads = [], []
    for head in range(2):
        keys = extend_keys(k_float, lane, head, step * rows, length_ref[0])
        values = extend_values(v_float, lane, head)
        query, grad = extended_ref[head], grads[head]
        probs = jnp.exp(times_rows(keys, query))
        score_grad = (probs * times_rows(values, grad)).astype(jnp.bfloat16)
        value_grads.append(matmul(probs.astype(jnp.bfloat16), grad))
        key_grads.append(matmul(score_grad, query))
        own = slice(HD * head, HD * (head + 1))
        part = matmul(across[own], score_grad)

        @pl.when(step == 0)
        def _():
            turned[own, :] = part

        @pl.when(step > 0)
        def _():
            turned[own, :] += part

    here = pl.ds(pl.multiple_of(step * rows, rows), rows)
    key_grad = jnp.where(lane < HD, key_grads[0], key_grads[1])
    value_grad = jnp.where(lane < HD, value_grads[0], value_grads[1])
    out_ref[here, PAIR : 2 * PAIR] = key_grad.astype(jnp.bfloat16)
    out_ref[here, 2 * PAIR :] = value_grad.astype(jnp.bfloat16)

    @pl.when(step == pl.num_programs(0) - 1)
    def _():
        def finish(j, carry):
            here = pl.ds(pl.multiple_of(j * rows, rows), rows)
            out_ref[here, :PAIR] = (turned[:, here].T * HD**-0.5).astype(jnp.bfloat16)
            return carry

        lax.fori_loop(0, seq_len // rows, finish, 0)


def attend_backward(length, extended, qkv, context, context_grad, pair):
    seq_len = qkv.shape[0]
    rows = min(256, seq_len)
    return pl.pallas_call(
        backward_kernel,
        grid_spec=pltpu.PrefetchScalarGridSpec(
            num_scalar_prefetch=1,
            grid=(seq_len // rows,),
            in_specs=[
                pl.BlockSpec((2, seq_len, PAIR), lambda i, n: (pair, 0, 0)),
                pl.BlockSpec((rows, PAIR), lambda i, n: (i, 3 * pair + 1)),
                pl.BlockSpec((rows, PAIR), lambda i, n: (i, 3 * pair + 2)),
                pl.BlockSpec((seq_len, PAIR), lambda i, n: (0, pair)),
                pl.BlockSpec((seq_len, PAIR), lambda i, n: (0, pair)),
            ],
            out_specs=pl.BlockSpec((seq_len, 3 * PAIR), lambda i, n: (0, 0)),
            scratch_shapes=[
                pltpu.VMEM((2, seq_len, PAIR), jnp.bfloat16),
                pltpu.VMEM((PAIR, seq_len), jnp.float32),
            ],
        ),
        out_shape=jax.ShapeDtypeStruct((seq_len, 3 * PAIR), jnp.bfloat16),
        compiler_params=pltpu.CompilerParams(vmem_limit_bytes=VMEM_BYTES),
        cost_estimate=pl.CostEstimate(
            flops=20 * seq_len * seq_len * 2 * PAIR,
            bytes_accessed=20 * seq_len * PAIR,
            transcendentals=2 * seq_len * seq_len,
        ),
        name="attend_backward",
    )(length, extended, qkv, qkv, context, context_grad)


def tie(*values):
    return lax.optimization_barrier(values)


def flip(array_in, axis_name, bits):
    size = lax.axis_size(axis_name)
    return lax.ppermute(array_in, axis_name, [(i, i ^ bits) for i in range(size)])


def total(array_in, axis_names):
    for name in axis_names:
        bits = 1
        while bits < lax.axis_size(name):
            array_in = array_in + flip(array_in, name, bits)
            bits *= 2
    return array_in


def shards(
    hidden_in,
    lengths,
    query_weight,
    query_bias,
    key_weight,
    value_weight,
    value_bias,
    output_weight,
    output_bias,
    first_gain,
    first_shift,
    inner_weight,
    inner_bias,
    outer_weight,
    outer_bias,
    second_gain,
    second_shift,
    cotangent,
    teacher,
):
    seq_len, model_width = hidden_in.shape
    ranks = lax.axis_size("tensor")
    rank = lax.axis_index("tensor")
    copies = lax.axis_size("dp")
    copy = lax.axis_index("dp")
    share_rows = seq_len // ranks
    heads_width = query_weight.shape[1]
    units = inner_weight.shape[1]
    pairs = heads_width // PAIR
    row_valid = jnp.arange(seq_len, dtype=jnp.int32) < lengths[0]

    def take_own(array_in):
        return lax.dynamic_slice_in_dim(array_in, rank * share_rows, share_rows, 0)

    def by_pairs(*arrays):
        return jnp.concatenate(
            [a[..., p * PAIR : (p + 1) * PAIR] for p in range(pairs) for a in arrays], axis=-1
        )

    def own_part(weight):
        rows = weight.shape[0] // copies
        return lax.dynamic_slice_in_dim(weight, copy * rows, rows, 0)

    def others(part):
        return jnp.stack([flip(part, "tensor", s) for s in range(1, ranks)])

    def gathered(parts):
        return lax.all_gather(parts, "dp", axis=1, tiled=True)

    def trade(blocks):
        return lax.all_to_all(blocks, "tensor", 0, 0)

    def block_of(blocks, s):
        return lax.dynamic_index_in_dim(blocks, rank ^ s, 0, keepdims=False)

    def reordered(blocks):
        return jnp.stack([block_of(blocks, s) for s in range(ranks)])

    def column_blocks(array_in):
        width = array_in.shape[1] // ranks
        return jnp.stack(
            [
                lax.dynamic_slice_in_dim(array_in, (rank ^ i) * width, width, 1)
                for i in range(ranks)
            ]
        )

    def add_blocks(blocks):
        return sum(blocks[i].astype(jnp.float32) for i in range(ranks))

    def ordered(vector_in):
        table = vector_in.reshape(ranks, -1)
        return jnp.concatenate(
            [lax.dynamic_index_in_dim(table, rank ^ s, 0, keepdims=False) for s in range(ranks)]
        )

    def half_columns(array_in, other):
        blocks = jnp.split(array_in, copies, axis=1)
        odd = ((copy & 1) ^ other) == 1
        return jnp.concatenate(
            [jnp.where(odd, blocks[i + 1], blocks[i]) for i in range(0, copies, 2)], axis=1
        )

    def half_rows(whole, other):
        blocks = whole.reshape(copies // 2, 2, -1, whole.shape[1])
        mine = lax.dynamic_index_in_dim(blocks, (copy & 1) ^ other, 1, keepdims=False)
        return mine.reshape(-1, whole.shape[1])

    def with_other_core(kept, given):
        come = flip(given, "dp", 1).astype(jnp.float32)
        return (kept.astype(jnp.float32) + come).astype(jnp.bfloat16)

    def qkv_product(qkv_low):
        return [matmul(half, qkv_low).astype(jnp.bfloat16) for half in hidden_halves]

    def halves_of(kept):
        places = list(range(1, copies.bit_length() - 1))
        states = []
        for part, order in zip(jnp.split(kept, 2, axis=1), (places[::-1], places)):
            states.append((part.reshape(copies // 2, -1, part.shape[1]), list(places), order))
        return states

    def begin(states):
        started = []
        for blocks, left, order in states:
            place = order[0]
            low = 2 ** sum(p < place for p in left)
            split = blocks.reshape(-1, 2, low, *blocks.shape[1:])
            mine = (copy >> place) & 1
            keep = lax.dynamic_index_in_dim(split, mine, 1, keepdims=False)
            give = lax.dynamic_index_in_dim(split, 1 - mine, 1, keepdims=False)
            started.append((keep, flip(give, "dp", 1 << place)))
        return started

    def complete(states, started):
        out = []
        for (blocks, left, order), (keep, come) in zip(states, started):
            added = keep.astype(jnp.float32) + come.astype(jnp.float32)
            added = added.astype(jnp.bfloat16).reshape(-1, *blocks.shape[1:])
            out.append((added, [p for p in left if p != order[0]], order[1:]))
        return out

    def step(states):
        return complete(states, begin(states))

    def finished(states):
        while states[0][2]:
            states = step(states)
        return jnp.concatenate([blocks[0] for blocks, _, _ in states], axis=1)

    def scatter_copies(whole):
        return lax.psum_scatter(whole, "dp", scatter_dimension=0, tiled=True)

    def column_sums(array_in):
        return jnp.sum(array_in.astype(jnp.float32), axis=0)

    qkv_weight = by_pairs(query_weight, key_weight, value_weight)
    qkv_bias = by_pairs(query_bias, jnp.zeros_like(query_bias), value_bias)
    output_part, both_part = own_part(output_weight), own_part(
        jnp.concatenate([inner_weight, outer_weight], axis=1)
    )
    part_rows = output_part.shape[0]
    bias_rows = inner_bias.reshape(-1, heads_width)
    output_part = jnp.concatenate([output_part, bias_rows, jnp.zeros_like(bias_rows)])
    output_parts = trade(jnp.broadcast_to(output_part, (ranks, *output_part.shape)))
    near_part = flip(both_part, "tensor", 1)
    qkv_part = own_part(qkv_weight)
    qkv = (matmul(hidden_in, qkv_weight) + qkv_bias).astype(jnp.bfloat16)
    output_parts, near_part, qkv = tie(output_parts, near_part, qkv)
    far_parts = [flip(both_part, "tensor", s) for s in range(2, ranks)]
    output_others = [block_of(output_parts, s) for s in range(1, ranks)]
    output_rest = [p[:part_rows] for p in output_others]
    biases = [p[part_rows : part_rows + bias_rows.shape[0]] for p in output_others]

    column = lax.broadcasted_iota(jnp.int32, (part_rows, PAIR), 1)
    digits = jnp.where(column == 0, lengths[0] // 256, lengths[0] % 256).astype(jnp.bfloat16)
    near_rows = lax.all_gather(
        jnp.concatenate([near_part, *output_rest, digits], axis=1), "dp", axis=0, tiled=True
    )
    context, extended = attend_forward(lengths, qkv)
    received = trade(context.reshape(ranks, share_rows, heads_width))
    far_parts, context, hidden_late = tie(far_parts, context, hidden_in)
    far_rows = gathered(jnp.stack(far_parts))
    hidden_halves = [half_columns(hidden_late, other).T for other in range(2)]
    received, hidden_halves = tie(received, hidden_halves)
    digits = near_rows[::part_rows, -PAIR:].astype(jnp.float32)
    token_total = jnp.sum(256.0 * digits[:, 0] + digits[:, 1])
    grad_scale = seq_len * copies / (2.0 * token_total)
    context_all = jnp.concatenate(
        [block_of(received, s) for s in range(ranks)], axis=1
    )
    both_rest = [near_rows[:, : 2 * units]] + [far_rows[i] for i in range(ranks - 2)]
    inner_weights = [inner_weight] + [rest[:, :units] for rest in both_rest]
    outer_weights = [outer_weight] + [rest[:, units:] for rest in both_rest]
    inner_biases = [inner_bias] + [b.reshape(-1) for b in biases]
    output_weight_all = jnp.concatenate([output_weight, near_rows[:, 2 * units : -PAIR]], axis=1)

    hidden_own = take_own(hidden_in).astype(jnp.float32)
    attention = times_rows(context_all, output_weight_all)
    normed, normal_one, inverse_one = layer_norm(
        hidden_own + (attention + output_bias), first_gain, first_shift
    )
    normed_low = normed.astype(jnp.bfloat16)
    activated, slopes = [], []
    branch = outer_bias.astype(jnp.float32)
    for s in range(ranks):
        value, slope = gelu_parts(matmul(normed_low, inner_weights[s]) + inner_biases[s])
        activated.append(value.astype(jnp.bfloat16))
        slopes.append(slope.astype(jnp.bfloat16))
        branch = branch + times_rows(activated[s], outer_weights[s])
    final, normal_two, inverse_two = layer_norm(normed + branch, second_gain, second_shift)
    row_mask = take_own(row_valid)[:, None]
    difference = final - take_own(teacher).astype(jnp.float32)
    loss_part = jnp.sum(jnp.where(row_mask, difference * difference, 0.0))
    final_grad = jnp.where(
        row_mask, take_own(cotangent).astype(jnp.float32) + grad_scale * difference, 0.0
    )
    second_grad = norm_back(final_grad, normal_two, inverse_two, second_gain)
    branch_low = second_grad.astype(jnp.bfloat16)
    outer_whole = over_rows(branch_low, jnp.concatenate(activated, axis=1)).astype(jnp.bfloat16)
    outer_whole, branch_low, qkv_part = tie(outer_whole, branch_low, qkv_part)
    outer_rows = scatter_copies(outer_whole)
    qkv_parts = others(qkv_part)
    inner_lows = []
    normed_grad = second_grad
    for s in range(ranks):
        inner_low = (matmul(branch_low, outer_weights[s]) * slopes[s]).astype(jnp.bfloat16)
        inner_lows.append(inner_low)
        normed_grad = normed_grad + times_rows(inner_low, inner_weights[s])
    first_grad = norm_back(normed_grad, normal_one, inverse_one, first_gain)
    attention_low = first_grad.astype(jnp.bfloat16)
    grad_all = matmul(attention_low, output_weight_all).astype(jnp.bfloat16)
    grad_all, inner_lows, qkv_parts = tie(grad_all, inner_lows, qkv_parts)
    qkv_rest = gathered(qkv_parts)
    context_grad = trade(column_blocks(grad_all)).reshape(seq_len, heads_width)
    inner_whole = over_rows(normed_low, jnp.concatenate(inner_lows, axis=1)).astype(jnp.bfloat16)
    inner_kept = with_other_core(half_rows(inner_whole, 0), half_rows(inner_whole, 1))
    output_whole = over_rows(attention_low, context_all).astype(jnp.bfloat16)
    inner_states = halves_of(inner_kept)
    inner_started = begin(inner_states)
    vectors = [
        ordered(jnp.concatenate([column_sums(low) for low in inner_lows])),
        column_sums(attention_low),
        column_sums(normed_grad * normal_one),
        column_sums(normed_grad),
        column_sums(branch_low),
        column_sums(final_grad * normal_two),
        column_sums(final_grad),
        ordered(column_sums(grad_all)),
        jnp.full((model_width,), loss_part),
    ]
    vectors = jnp.concatenate([v.reshape(-1, model_width) for v in vectors])
    vectors = vectors + flip(vectors, "dp", 1)
    context_grad, inner_kept, vectors, output_whole = tie(
        context_grad, inner_kept, vectors, output_whole
    )
    output_rows = scatter_copies(output_whole)
    outer_come = trade(column_blocks(outer_rows))
    rank_bits = [1 << p for p in range(ranks.bit_length() - 1)]
    vector_come = flip(vectors, "tensor", rank_bits[0])

    def add_input(rows, moved, pair):
        columns = slice(3 * PAIR * pair, 3 * PAIR * (pair + 1))
        blocks = jnp.concatenate([block_of(moved, s) for s in range(ranks)], axis=1)
        weights = [qkv_weight] + [qkv_rest[s] for s in range(ranks - 1)]
        return rows + times_rows(blocks, jnp.concatenate([w[:, columns] for w in weights], axis=1))

    input_rows = first_grad
    query_sums = []
    for pair in range(pairs):
        qkv_low = attend_backward(lengths, extended, qkv, context, context_grad, pair)
        if pair == 0:
            qkv_low, inner_started, outer_come, vector_come = tie(
                qkv_low, inner_started, outer_come, vector_come
            )
            outer_weight_grad = add_blocks(outer_come)
            inner_states = complete(inner_states, inner_started)
            inner_started = begin(inner_states) if inner_states[0][2] else None
            vectors = vectors + vector_come
            vector_come = flip(vectors, "tensor", rank_bits[1])
        if pair == 0:
            qkv_kept = [with_other_core(*qkv_product(qkv_low))]
            context_grad, qkv_kept = tie(context_grad, qkv_kept)
        else:
            moved, qkv_low, inner_started, vector_come, output_rows, qkv_rest = tie(
                moved, qkv_low, inner_started, vector_come, output_rows, qkv_rest
            )
            vectors = vectors + vector_come
            input_rows = add_input(input_rows, moved, pair - 1)
            qkv_kept.append(with_other_core(*qkv_product(qkv_low)))
        moved = trade(qkv_low.reshape(ranks, share_rows, -1))
        query_sums.append(column_sums(qkv_low[:, :PAIR]))
    inner_states = complete(inner_states, inner_started)
    inner_parts = finished(inner_states)
    if pairs == 1:
        vectors = vectors + vector_come
    for bit in rank_bits[2:]:
        vectors = vectors + flip(vectors, "tensor", bit)
    query_sums = jnp.concatenate(query_sums)
    query_sums = query_sums + flip(query_sums, "dp", 1)
    query_row = jnp.pad(query_sums, (0, model_width - heads_width))[None]
    vectors = jnp.concatenate([vectors, query_row])
    for place in range(1, copies.bit_length() - 1):
        vectors = vectors + flip(vectors, "dp", 1 << place)
    query_sums = vectors[-1, :heads_width]

    high = query_sums.astype(jnp.bfloat16)
    middle = (query_sums - high.astype(jnp.float32)).astype(jnp.bfloat16)
    low = query_sums - high.astype(jnp.float32) - middle.astype(jnp.float32)
    digit_rows = jnp.stack([high, middle, low.astype(jnp.bfloat16)])
    digit_rows = jnp.pad(digit_rows, ((0, 5), (units, 0)))
    rows = [inner_parts, output_rows]
    rows = [[jnp.split(r, ranks, axis=1)[s] for r in rows] for s in range(ranks)]
    last = [jnp.concatenate([jnp.concatenate(r, axis=1), digit_rows]) for r in rows]
    last = reordered(jnp.stack(last))
    moved, qkv_kept, last = tie(moved, qkv_kept, last)
    qkv_sums = finished(halves_of(jnp.concatenate(qkv_kept, axis=1)))
    input_rows = add_input(input_rows, moved, pairs - 1)
    last = trade(last)
    both_sum = add_blocks(last[:, :part_rows])
    inner_weight_grad, output_weight_grad = both_sum[:, :units], both_sum[:, units:]
    digit_rows = last[:, part_rows:, units:].astype(jnp.float32)
    query_bias_grad = (digit_rows[:, 0] + digit_rows[:, 1] + digit_rows[:, 2]).reshape(-1)
    qkv_sums = jnp.split(qkv_sums.astype(jnp.float32), 3 * pairs, axis=1)
    query_weight_grad, key_weight_grad, value_weight_grad = [
        jnp.concatenate(qkv_sums[i::3], axis=1) for i in range(3)
    ]

    wide = ranks * units // model_width
    inner_bias_grad = vectors[:wide].reshape(-1)
    (
        output_bias_grad,
        first_gain_grad,
        first_shift_grad,
        outer_bias_grad,
        second_gain_grad,
        second_shift_grad,
        value_bias_grad,
    ) = [vectors[wide + i] for i in range(7)]
    return (
        final.astype(jnp.bfloat16),
        vectors[wide + 7, 0] / token_total,
        input_rows,
        query_weight_grad,
        query_bias_grad,
        key_weight_grad,
        value_weight_grad,
        value_bias_grad,
        output_weight_grad,
        output_bias_grad,
        first_gain_grad,
        first_shift_grad,
        inner_weight_grad,
        inner_bias_grad,
        outer_weight_grad,
        outer_bias_grad,
        second_gain_grad,
        second_shift_grad,
    )


def solution(mesh):
    rows, columns, split = P("dp", None), P(None, "tensor"), P("dp", "tensor")
    part, whole, own = P("tensor"), P(), P(("dp", "tensor"), None)
    in_specs = (
        rows,
        P("dp"),
        columns,
        part,
        columns,
        columns,
        part,
        columns,
        whole,
        whole,
        whole,
        columns,
        part,
        columns,
        whole,
        whole,
        whole,
        rows,
        rows,
    )
    out_specs = (
        own,
        whole,
        own,
        split,
        whole,
        split,
        split,
        whole,
        split,
        whole,
        whole,
        whole,
        split,
        whole,
        split,
        whole,
        whole,
        whole,
    )
    return jax.shard_map(shards, mesh=mesh, in_specs=in_specs, out_specs=out_specs, check_vma=False)
```

```python
import jax
import jax.numpy as jnp
from jax import lax
from jax.experimental import pallas as pl
from jax.experimental.pallas import tpu as pltpu
from jax.sharding import PartitionSpec as P

HD = 64
PAIR = 128
VMEM_BYTES = 60000 * 1024


epsilon = 1e-05


def matmul(former, latter):
    return jnp.dot(former, latter, preferred_element_type=jnp.float32)


def times_rows(former, latter):
    return lax.dot_general(
        former, latter, (((1,), (1,)), ((), ())), preferred_element_type=jnp.float32
    )


def over_rows(former, latter):
    return lax.dot_general(
        former, latter, (((0,), (0,)), ((), ())), preferred_element_type=jnp.float32
    )


def layer_norm(hidden, norm_gain, norm_shift):
    centered = hidden - jnp.mean(hidden, axis=-1, keepdims=True)
    inverse = lax.rsqrt(jnp.mean(centered * centered, axis=-1, keepdims=True) + epsilon)
    normal = centered * inverse
    return (normal * norm_gain + norm_shift, normal, inverse)


def norm_back(upstream, normal, inverse, norm_gain):
    scaled = upstream * norm_gain
    return inverse * (
        scaled
        - jnp.mean(scaled, axis=-1, keepdims=True)
        - normal * jnp.mean(scaled * normal, axis=-1, keepdims=True)
    )


def gelu_parts(values):
    cumulative = 0.5 * (1.0 + jax.scipy.special.erf(values * 0.7071067811865476))
    slope = cumulative + values * jnp.exp(-0.5 * values * values) * 0.3989422804014327
    return (values * cumulative, slope)


def lanes(rows):
    return lax.broadcasted_iota(jnp.int32, (rows, PAIR), 1)


def in_head(lane, head):
    return (lane < HD) if head == 0 else (lane >= HD)


def extend(base, lane, head, first, offset):
    start = HD * (1 - head)
    high = offset.astype(jnp.bfloat16).astype(jnp.float32)
    middle = (offset - high).astype(jnp.bfloat16).astype(jnp.float32)
    out = jnp.where(lane == start, first, 0.0)
    out = jnp.where(lane == start + 1, -high, out)
    out = jnp.where(lane == start + 2, -middle, out)
    out = jnp.where(lane == start + 3, high + middle - offset, out)
    return jnp.where(in_head(lane, head), base, out).astype(jnp.bfloat16)


def extend_keys(keys, lane, head, row_start, length):
    start = HD * (1 - head)
    position = row_start + lax.broadcasted_iota(jnp.int32, keys.shape, 0)
    bias = jnp.where(position < length, 0.0, -1e30)
    ones = jnp.where((lane > start) & (lane < start + 4), 1.0, 0.0)
    side = jnp.where(lane == start, bias, ones)
    return jnp.where(in_head(lane, head), keys, side).astype(jnp.bfloat16)


def extend_values(values, lane, head):
    return jnp.where(in_head(lane, head), values, 1.0).astype(jnp.bfloat16)


def forward_kernel(length_ref, q_ref, k_ref, v_ref, context_ref, extended_ref, keys, values):
    @pl.when(pl.program_id(1) == 0)
    def _():
        lane = lanes(k_ref.shape[0])
        k_float = k_ref[...].astype(jnp.float32)
        v_float = v_ref[...].astype(jnp.float32)
        for head in range(2):
            keys[head] = extend_keys(k_float, lane, head, 0, length_ref[0])
            values[head] = extend_values(v_float, lane, head)

    lane = lanes(q_ref.shape[0])
    scaled = q_ref[...].astype(jnp.float32) * HD**-0.5
    contexts = []
    for head in range(2):
        plain = jnp.where(lane == HD * (1 - head), 1.0, 0.0)
        query = jnp.where(in_head(lane, head), scaled, plain).astype(jnp.bfloat16)
        scores = times_rows(query, keys[head])
        peak = jnp.max(scores, axis=1, keepdims=True)
        exponent = jnp.exp(scores - peak).astype(jnp.bfloat16)
        out = matmul(exponent, values[head])
        contexts.append(out / pltpu.roll(out, HD, 1))
        extended_ref[head] = extend(scaled, lane, head, 1.0, peak + jnp.log(out))
    context_ref[...] = jnp.where(lane < HD, contexts[0], contexts[1]).astype(jnp.bfloat16)


def attend_forward(length, qkv):
    seq_len = qkv.shape[0]
    pairs = qkv.shape[1] // (3 * PAIR)
    rows = min(256, seq_len)
    return pl.pallas_call(
        forward_kernel,
        grid_spec=pltpu.PrefetchScalarGridSpec(
            num_scalar_prefetch=1,
            grid=(pairs, seq_len // rows),
            in_specs=[
                pl.BlockSpec((rows, PAIR), lambda p, i, n: (i, 3 * p)),
                pl.BlockSpec((seq_len, PAIR), lambda p, i, n: (0, 3 * p + 1)),
                pl.BlockSpec((seq_len, PAIR), lambda p, i, n: (0, 3 * p + 2)),
            ],
            out_specs=[
                pl.BlockSpec((rows, PAIR), lambda p, i, n: (i, p)),
                pl.BlockSpec((2, rows, PAIR), lambda p, i, n: (p, i, 0)),
            ],
            scratch_shapes=[pltpu.VMEM((2, seq_len, PAIR), jnp.bfloat16)] * 2,
        ),
        out_shape=[
            jax.ShapeDtypeStruct((seq_len, pairs * PAIR), jnp.bfloat16),
            jax.ShapeDtypeStruct((2 * pairs, seq_len, PAIR), jnp.bfloat16),
        ],
        compiler_params=pltpu.CompilerParams(vmem_limit_bytes=VMEM_BYTES),
        cost_estimate=pl.CostEstimate(
            flops=8 * seq_len * seq_len * 2 * PAIR * pairs,
            bytes_accessed=12 * seq_len * PAIR * pairs,
            transcendentals=2 * seq_len * seq_len * pairs,
        ),
        name="attend_forward",
    )(length, qkv, qkv, qkv)


def backward_kernel(length_ref, extended_ref, k_ref, v_ref, context_ref, grad_ref, out_ref, grads, turned):
    step = pl.program_id(0)
    seq_len, rows = grad_ref.shape[0], k_ref.shape[0]

    @pl.when(step == 0)
    def _():
        def prepare(j, carry):
            here = pl.ds(pl.multiple_of(j * rows, rows), rows)
            lane = lanes(rows)
            grad = grad_ref[here, :].astype(jnp.float32)
            product = grad * context_ref[here, :].astype(jnp.float32)
            for head in range(2):
                centre = jnp.sum(
                    jnp.where(in_head(lane, head), product, 0.0), axis=1, keepdims=True
                )
                grads[head, here, :] = extend(grad, lane, head, 0.0, centre)
            return carry

        lax.fori_loop(0, seq_len // rows, prepare, 0)

    lane = lanes(rows)
    k_float = k_ref[...].astype(jnp.float32)
    v_float = v_ref[...].astype(jnp.float32)
    across = k_float.T.astype(jnp.bfloat16)
    key_grads, value_grads = [], []
    for head in range(2):
        keys = extend_keys(k_float, lane, head, step * rows, length_ref[0])
        values = extend_values(v_float, lane, head)
        query, grad = extended_ref[head], grads[head]
        probs = jnp.exp(times_rows(keys, query))
        score_grad = (probs * times_rows(values, grad)).astype(jnp.bfloat16)
        value_grads.append(matmul(probs.astype(jnp.bfloat16), grad))
        key_grads.append(matmul(score_grad, query))
        own = slice(HD * head, HD * (head + 1))
        part = matmul(across[own], score_grad)

        @pl.when(step == 0)
        def _():
            turned[own, :] = part

        @pl.when(step > 0)
        def _():
            turned[own, :] += part

    here = pl.ds(pl.multiple_of(step * rows, rows), rows)
    key_grad = jnp.where(lane < HD, key_grads[0], key_grads[1])
    value_grad = jnp.where(lane < HD, value_grads[0], value_grads[1])
    out_ref[here, PAIR : 2 * PAIR] = key_grad.astype(jnp.bfloat16)
    out_ref[here, 2 * PAIR :] = value_grad.astype(jnp.bfloat16)

    @pl.when(step == pl.num_programs(0) - 1)
    def _():
        def finish(j, carry):
            here = pl.ds(pl.multiple_of(j * rows, rows), rows)
            out_ref[here, :PAIR] = (turned[:, here].T * HD**-0.5).astype(jnp.bfloat16)
            return carry

        lax.fori_loop(0, seq_len // rows, finish, 0)


def attend_backward(length, extended, qkv, context, context_grad, pair):
    seq_len = qkv.shape[0]
    rows = min(256, seq_len)
    return pl.pallas_call(
        backward_kernel,
        grid_spec=pltpu.PrefetchScalarGridSpec(
            num_scalar_prefetch=1,
            grid=(seq_len // rows,),
            in_specs=[
                pl.BlockSpec((2, seq_len, PAIR), lambda i, n: (pair, 0, 0)),
                pl.BlockSpec((rows, PAIR), lambda i, n: (i, 3 * pair + 1)),
                pl.BlockSpec((rows, PAIR), lambda i, n: (i, 3 * pair + 2)),
                pl.BlockSpec((seq_len, PAIR), lambda i, n: (0, pair)),
                pl.BlockSpec((seq_len, PAIR), lambda i, n: (0, pair)),
            ],
            out_specs=pl.BlockSpec((seq_len, 3 * PAIR), lambda i, n: (0, 0)),
            scratch_shapes=[
                pltpu.VMEM((2, seq_len, PAIR), jnp.bfloat16),
                pltpu.VMEM((PAIR, seq_len), jnp.float32),
            ],
        ),
        out_shape=jax.ShapeDtypeStruct((seq_len, 3 * PAIR), jnp.bfloat16),
        compiler_params=pltpu.CompilerParams(vmem_limit_bytes=VMEM_BYTES),
        cost_estimate=pl.CostEstimate(
            flops=20 * seq_len * seq_len * 2 * PAIR,
            bytes_accessed=20 * seq_len * PAIR,
            transcendentals=2 * seq_len * seq_len,
        ),
        name="attend_backward",
    )(length, extended, qkv, qkv, context, context_grad)


def tie(*values):
    return lax.optimization_barrier(values)


def flip(array_in, axis_name, bits):
    size = lax.axis_size(axis_name)
    return lax.ppermute(array_in, axis_name, [(i, i ^ bits) for i in range(size)])


def total(array_in, axis_names):
    for name in axis_names:
        bits = 1
        while bits < lax.axis_size(name):
            array_in = array_in + flip(array_in, name, bits)
            bits *= 2
    return array_in


def shards(
    hidden_in,
    lengths,
    query_weight,
    query_bias,
    key_weight,
    value_weight,
    value_bias,
    output_weight,
    output_bias,
    first_gain,
    first_shift,
    inner_weight,
    inner_bias,
    outer_weight,
    outer_bias,
    second_gain,
    second_shift,
    cotangent,
    teacher,
):
    seq_len, model_width = hidden_in.shape
    ranks = lax.axis_size("tensor")
    rank = lax.axis_index("tensor")
    copies = lax.axis_size("dp")
    copy = lax.axis_index("dp")
    share_rows = seq_len // ranks
    heads_width = query_weight.shape[1]
    units = inner_weight.shape[1]
    pairs = heads_width // PAIR
    row_valid = jnp.arange(seq_len, dtype=jnp.int32) < lengths[0]

    def take_own(array_in):
        return lax.dynamic_slice_in_dim(array_in, rank * share_rows, share_rows, 0)

    def by_pairs(*arrays):
        return jnp.concatenate(
            [a[..., p * PAIR : (p + 1) * PAIR] for p in range(pairs) for a in arrays], axis=-1
        )

    def own_part(weight):
        rows = weight.shape[0] // copies
        return lax.dynamic_slice_in_dim(weight, copy * rows, rows, 0)

    def others(part):
        return jnp.stack([flip(part, "tensor", s) for s in range(1, ranks)])

    def gathered(parts):
        return lax.all_gather(parts, "dp", axis=1, tiled=True)

    def trade(blocks):
        return lax.all_to_all(blocks, "tensor", 0, 0)

    def block_of(blocks, s):
        return lax.dynamic_index_in_dim(blocks, rank ^ s, 0, keepdims=False)

    def reordered(blocks):
        return jnp.stack([block_of(blocks, s) for s in range(ranks)])

    def column_blocks(array_in):
        width = array_in.shape[1] // ranks
        return jnp.stack(
            [
                lax.dynamic_slice_in_dim(array_in, (rank ^ i) * width, width, 1)
                for i in range(ranks)
            ]
        )

    def add_blocks(blocks):
        return sum(blocks[i].astype(jnp.float32) for i in range(ranks))

    def ordered(vector_in):
        table = vector_in.reshape(ranks, -1)
        return jnp.concatenate(
            [lax.dynamic_index_in_dim(table, rank ^ s, 0, keepdims=False) for s in range(ranks)]
        )

    def half_columns(array_in, other):
        blocks = jnp.split(array_in, copies, axis=1)
        odd = ((copy & 1) ^ other) == 1
        return jnp.concatenate(
            [jnp.where(odd, blocks[i + 1], blocks[i]) for i in range(0, copies, 2)], axis=1
        )

    def half_rows(whole, other):
        blocks = whole.reshape(copies // 2, 2, -1, whole.shape[1])
        mine = lax.dynamic_index_in_dim(blocks, (copy & 1) ^ other, 1, keepdims=False)
        return mine.reshape(-1, whole.shape[1])

    def with_other_core(kept, given):
        come = flip(given, "dp", 1).astype(jnp.float32)
        return (kept.astype(jnp.float32) + come).astype(jnp.bfloat16)

    def qkv_product(qkv_low):
        return [matmul(half, qkv_low).astype(jnp.bfloat16) for half in hidden_halves]

    def to_chips(kept):
        blocks = [part.reshape(copies // 2, -1, part.shape[1]) for part in kept]
        rows = []
        for t in range(copies // 2):
            pieces = [
                lax.dynamic_index_in_dim(b, (copy >> 1) ^ t, 0, keepdims=False) for b in blocks
            ]
            rows.append(jnp.concatenate(pieces, axis=1))
        return [rows[0]] + [flip(rows[t], "dp", 2 * t) for t in range(1, copies // 2)]

    def add_all(parts):
        return sum(part.astype(jnp.float32) for part in parts)

    def scatter_copies(whole):
        return lax.psum_scatter(whole, "dp", scatter_dimension=0, tiled=True)

    def column_sums(array_in):
        return jnp.sum(array_in.astype(jnp.float32), axis=0)

    qkv_weight = by_pairs(query_weight, key_weight, value_weight)
    qkv_bias = by_pairs(query_bias, jnp.zeros_like(query_bias), value_bias)
    output_part, both_part = own_part(output_weight), own_part(
        jnp.concatenate([inner_weight, outer_weight], axis=1)
    )
    part_rows = output_part.shape[0]
    bias_rows = inner_bias.reshape(-1, heads_width)
    output_part = jnp.concatenate([output_part, bias_rows, jnp.zeros_like(bias_rows)])
    output_parts = trade(jnp.broadcast_to(output_part, (ranks, *output_part.shape)))
    near_part = flip(both_part, "tensor", 1)
    qkv_part = own_part(qkv_weight)
    qkv = (matmul(hidden_in, qkv_weight) + qkv_bias).astype(jnp.bfloat16)
    output_parts, near_part, qkv = tie(output_parts, near_part, qkv)
    far_parts = [flip(both_part, "tensor", s) for s in range(2, ranks)]
    output_others = [block_of(output_parts, s) for s in range(1, ranks)]
    output_rest = [p[:part_rows] for p in output_others]
    biases = [p[part_rows : part_rows + bias_rows.shape[0]] for p in output_others]

    column = lax.broadcasted_iota(jnp.int32, (part_rows, PAIR), 1)
    digits = jnp.where(column == 0, lengths[0] // 256, lengths[0] % 256).astype(jnp.bfloat16)
    near_rows = lax.all_gather(
        jnp.concatenate([near_part, *output_rest, digits], axis=1), "dp", axis=0, tiled=True
    )
    context, extended = attend_forward(lengths, qkv)
    received = trade(context.reshape(ranks, share_rows, heads_width))
    far_parts, context, hidden_late = tie(far_parts, context, hidden_in)
    far_rows = gathered(jnp.stack([p[:, i : i + units] for p in far_parts for i in (0, units)]))
    hidden_halves = [half_columns(hidden_late, other).T for other in range(2)]
    received, hidden_halves = tie(received, hidden_halves)
    digits = near_rows[::part_rows, -PAIR:].astype(jnp.float32)
    token_total = jnp.sum(256.0 * digits[:, 0] + digits[:, 1])
    grad_scale = seq_len * copies / (2.0 * token_total)
    context_all = jnp.concatenate(
        [block_of(received, s) for s in range(ranks)], axis=1
    )
    inner_weights = [inner_weight, near_rows[:, :units]]
    outer_weights = [outer_weight, near_rows[:, units : 2 * units]]
    for i in range(ranks - 2):
        inner_weights.append(far_rows[2 * i])
        outer_weights.append(far_rows[2 * i + 1])
    inner_biases = [inner_bias] + [b.reshape(-1) for b in biases]
    output_weight_all = jnp.concatenate([output_weight, near_rows[:, 2 * units : -PAIR]], axis=1)

    hidden_own = take_own(hidden_in).astype(jnp.float32)
    attention = times_rows(context_all, output_weight_all)
    normed, normal_one, inverse_one = layer_norm(
        hidden_own + (attention + output_bias), first_gain, first_shift
    )
    normed_low = normed.astype(jnp.bfloat16)
    activated, slopes = [], []
    branch = outer_bias.astype(jnp.float32)
    for s in range(ranks):
        value, slope = gelu_parts(matmul(normed_low, inner_weights[s]) + inner_biases[s])
        activated.append(value.astype(jnp.bfloat16))
        slopes.append(slope.astype(jnp.bfloat16))
        branch = branch + times_rows(activated[s], outer_weights[s])
    final, normal_two, inverse_two = layer_norm(normed + branch, second_gain, second_shift)
    row_mask = take_own(row_valid)[:, None]
    difference = final - take_own(teacher).astype(jnp.float32)
    loss_part = jnp.sum(jnp.where(row_mask, difference * difference, 0.0))
    final_grad = jnp.where(
        row_mask, take_own(cotangent).astype(jnp.float32) + grad_scale * difference, 0.0
    )
    second_grad = norm_back(final_grad, normal_two, inverse_two, second_gain)
    branch_low = second_grad.astype(jnp.bfloat16)
    outer_whole = over_rows(branch_low, jnp.concatenate(activated, axis=1)).astype(jnp.bfloat16)
    outer_whole, branch_low, qkv_part = tie(outer_whole, branch_low, qkv_part)
    outer_rows = scatter_copies(outer_whole)
    qkv_parts = others(qkv_part)
    inner_lows = []
    normed_grad = second_grad
    for s in range(ranks):
        inner_low = (matmul(branch_low, outer_weights[s]) * slopes[s]).astype(jnp.bfloat16)
        inner_lows.append(inner_low)
        normed_grad = normed_grad + times_rows(inner_low, inner_weights[s])
    first_grad = norm_back(normed_grad, normal_one, inverse_one, first_gain)
    attention_low = first_grad.astype(jnp.bfloat16)
    grad_all = matmul(attention_low, output_weight_all).astype(jnp.bfloat16)
    grad_all, inner_lows, qkv_parts = tie(grad_all, inner_lows, qkv_parts)
    context_grad = trade(column_blocks(grad_all)).reshape(seq_len, heads_width)
    inner_whole = over_rows(normed_low, jnp.concatenate(inner_lows, axis=1)).astype(jnp.bfloat16)
    inner_kept = [
        with_other_core(half_rows(half, 0), half_rows(half, 1))
        for half in jnp.split(inner_whole, 2, axis=1)
    ]
    output_whole = over_rows(attention_low, context_all).astype(jnp.bfloat16)
    inner_chips = to_chips(inner_kept)
    vectors = [
        ordered(jnp.concatenate([column_sums(low) for low in inner_lows])),
        column_sums(attention_low),
        column_sums(normed_grad * normal_one),
        column_sums(normed_grad),
        column_sums(branch_low),
        column_sums(final_grad * normal_two),
        column_sums(final_grad),
        ordered(column_sums(grad_all)),
        jnp.full((model_width,), loss_part),
    ]
    vectors = jnp.concatenate([v.reshape(-1, model_width) for v in vectors])
    vectors = vectors + flip(vectors, "dp", 1)
    outer_blocks = column_blocks(outer_rows)
    context_grad, vectors, output_whole, outer_blocks = tie(
        context_grad, vectors, output_whole, outer_blocks
    )
    outer_come = trade(outer_blocks)
    rank_bits = [1 << p for p in range(ranks.bit_length() - 1)]
    vector_come = flip(vectors, "tensor", rank_bits[0])

    def add_input(rows, moved, pair):
        columns = slice(3 * PAIR * pair, 3 * PAIR * (pair + 1))
        blocks = jnp.concatenate([block_of(moved, s) for s in range(ranks)], axis=1)
        weights = [qkv_weight] + [qkv_rest[s] for s in range(ranks - 1)]
        return rows + times_rows(blocks, jnp.concatenate([w[:, columns] for w in weights], axis=1))

    input_rows = first_grad
    query_sums = []
    for pair in range(pairs):
        qkv_low = attend_backward(lengths, extended, qkv, context, context_grad, pair)
        if pair == 0:
            qkv_low, inner_chips, outer_come, vector_come, qkv_parts, output_whole = tie(
                qkv_low, inner_chips, outer_come, vector_come, qkv_parts, output_whole
            )
            output_rows = scatter_copies(output_whole)
            qkv_rest = gathered(qkv_parts)
            inner_rows = add_all(inner_chips).astype(jnp.bfloat16)
            inner_parts = jnp.split(inner_rows, ranks, axis=1)
            vectors = vectors + vector_come
            vector_come = flip(vectors, "tensor", rank_bits[1])
        if pair == 0:
            qkv_kept = [with_other_core(*qkv_product(qkv_low))]
            context_grad, qkv_kept, inner_parts = tie(context_grad, qkv_kept, inner_parts)
            inner_come = [flip(inner_parts[t], "tensor", t) for t in range(1, ranks)]
        else:
            moved, qkv_low, inner_come, vector_come, output_rows, qkv_kept = tie(
                moved, qkv_low, inner_come, vector_come, output_rows, qkv_kept
            )
            vectors = vectors + vector_come
            input_rows = add_input(input_rows, moved, pair - 1)
            qkv_kept.append(with_other_core(*qkv_product(qkv_low)))
        moved = trade(qkv_low.reshape(ranks, share_rows, -1))
        query_sums.append(column_sums(qkv_low[:, :PAIR]))
    if pairs == 1:
        vectors = vectors + vector_come
    for bit in rank_bits[2:]:
        vectors = vectors + flip(vectors, "tensor", bit)
    query_sums = jnp.concatenate(query_sums)
    query_sums = query_sums + flip(query_sums, "dp", 1)
    query_row = jnp.pad(query_sums, (0, model_width - heads_width))[None]
    vectors = jnp.concatenate([vectors, query_row])
    for place in range(1, copies.bit_length() - 1):
        vectors = vectors + flip(vectors, "dp", 1 << place)
    query_sums = vectors[-1, :heads_width]

    high = query_sums.astype(jnp.bfloat16)
    middle = (query_sums - high.astype(jnp.float32)).astype(jnp.bfloat16)
    low = query_sums - high.astype(jnp.float32) - middle.astype(jnp.float32)
    digit_rows = jnp.stack([high, middle, low.astype(jnp.bfloat16)])
    digit_rows = jnp.pad(digit_rows, ((0, 5), (0, 0)))
    last = [jnp.concatenate([part, digit_rows]) for part in jnp.split(output_rows, ranks, axis=1)]
    last = reordered(jnp.stack(last))
    moved, last, outer_come, inner_come = tie(moved, last, outer_come, inner_come)
    outer_weight_grad = add_blocks(outer_come)
    inner_weight_grad = add_all([inner_parts[0], *inner_come])
    qkv_sums = add_all(to_chips(qkv_kept))
    input_rows = add_input(input_rows, moved, pairs - 1)
    last = trade(last)
    output_weight_grad = add_blocks(last[:, :part_rows])
    digit_rows = last[:, part_rows:].astype(jnp.float32)
    query_bias_grad = (digit_rows[:, 0] + digit_rows[:, 1] + digit_rows[:, 2]).reshape(-1)
    qkv_sums = jnp.split(qkv_sums, 3 * pairs, axis=1)
    query_weight_grad, key_weight_grad, value_weight_grad = [
        jnp.concatenate(qkv_sums[i::3], axis=1) for i in range(3)
    ]

    wide = ranks * units // model_width
    inner_bias_grad = vectors[:wide].reshape(-1)
    (
        output_bias_grad,
        first_gain_grad,
        first_shift_grad,
        outer_bias_grad,
        second_gain_grad,
        second_shift_grad,
        value_bias_grad,
    ) = [vectors[wide + i] for i in range(7)]
    return (
        final.astype(jnp.bfloat16),
        vectors[wide + 7, 0] / token_total,
        input_rows,
        query_weight_grad,
        query_bias_grad,
        key_weight_grad,
        value_weight_grad,
        value_bias_grad,
        output_weight_grad,
        output_bias_grad,
        first_gain_grad,
        first_shift_grad,
        inner_weight_grad,
        inner_bias_grad,
        outer_weight_grad,
        outer_bias_grad,
        second_gain_grad,
        second_shift_grad,
    )


def solution(mesh):
    rows, columns, split = P("dp", None), P(None, "tensor"), P("dp", "tensor")
    part, whole, own = P("tensor"), P(), P(("dp", "tensor"), None)
    in_specs = (
        rows,
        P("dp"),
        columns,
        part,
        columns,
        columns,
        part,
        columns,
        whole,
        whole,
        whole,
        columns,
        part,
        columns,
        whole,
        whole,
        whole,
        rows,
        rows,
    )
    out_specs = (
        own,
        whole,
        own,
        split,
        whole,
        split,
        split,
        whole,
        split,
        whole,
        whole,
        whole,
        split,
        whole,
        split,
        whole,
        whole,
        whole,
    )
    return jax.shard_map(shards, mesh=mesh, in_specs=in_specs, out_specs=out_specs, check_vma=False)
```

```python
import jax
import jax.numpy as jnp
from jax import lax
from jax.experimental import pallas as pl
from jax.experimental.pallas import tpu as pltpu
from jax.sharding import PartitionSpec as P

HD = 64
PAIR = 128
VMEM_BYTES = 60000 * 1024


epsilon = 1e-05


def matmul(former, latter):
    return jnp.dot(former, latter, preferred_element_type=jnp.float32)


def times_rows(former, latter):
    return lax.dot_general(
        former, latter, (((1,), (1,)), ((), ())), preferred_element_type=jnp.float32
    )


def over_rows(former, latter):
    return lax.dot_general(
        former, latter, (((0,), (0,)), ((), ())), preferred_element_type=jnp.float32
    )


def layer_norm(hidden, norm_gain, norm_shift):
    centered = hidden - jnp.mean(hidden, axis=-1, keepdims=True)
    inverse = lax.rsqrt(jnp.mean(centered * centered, axis=-1, keepdims=True) + epsilon)
    normal = centered * inverse
    return (normal * norm_gain + norm_shift, normal, inverse)


def norm_back(upstream, normal, inverse, norm_gain):
    scaled = upstream * norm_gain
    return inverse * (
        scaled
        - jnp.mean(scaled, axis=-1, keepdims=True)
        - normal * jnp.mean(scaled * normal, axis=-1, keepdims=True)
    )


def gelu_parts(values):
    cumulative = 0.5 * (1.0 + jax.scipy.special.erf(values * 0.7071067811865476))
    slope = cumulative + values * jnp.exp(-0.5 * values * values) * 0.3989422804014327
    return (values * cumulative, slope)


def lanes(rows):
    return lax.broadcasted_iota(jnp.int32, (rows, PAIR), 1)


def in_head(lane, head):
    return (lane < HD) if head == 0 else (lane >= HD)


def extend(base, lane, head, first, offset):
    start = HD * (1 - head)
    high = offset.astype(jnp.bfloat16).astype(jnp.float32)
    middle = (offset - high).astype(jnp.bfloat16).astype(jnp.float32)
    out = jnp.where(lane == start, first, 0.0)
    out = jnp.where(lane == start + 1, -high, out)
    out = jnp.where(lane == start + 2, -middle, out)
    out = jnp.where(lane == start + 3, high + middle - offset, out)
    return jnp.where(in_head(lane, head), base, out).astype(jnp.bfloat16)


def extend_keys(keys, lane, head, row_start, length):
    start = HD * (1 - head)
    position = row_start + lax.broadcasted_iota(jnp.int32, keys.shape, 0)
    bias = jnp.where(position < length, 0.0, -1e30)
    ones = jnp.where((lane > start) & (lane < start + 4), 1.0, 0.0)
    side = jnp.where(lane == start, bias, ones)
    return jnp.where(in_head(lane, head), keys, side).astype(jnp.bfloat16)


def extend_values(values, lane, head):
    return jnp.where(in_head(lane, head), values, 1.0).astype(jnp.bfloat16)


def forward_kernel(length_ref, q_ref, k_ref, v_ref, context_ref, extended_ref, keys, values):
    @pl.when(pl.program_id(1) == 0)
    def _():
        lane = lanes(k_ref.shape[0])
        k_float = k_ref[...].astype(jnp.float32)
        v_float = v_ref[...].astype(jnp.float32)
        for head in range(2):
            keys[head] = extend_keys(k_float, lane, head, 0, length_ref[0])
            values[head] = extend_values(v_float, lane, head)

    lane = lanes(q_ref.shape[0])
    scaled = q_ref[...].astype(jnp.float32) * HD**-0.5
    contexts = []
    for head in range(2):
        plain = jnp.where(lane == HD * (1 - head), 1.0, 0.0)
        query = jnp.where(in_head(lane, head), scaled, plain).astype(jnp.bfloat16)
        scores = times_rows(query, keys[head])
        peak = jnp.max(scores, axis=1, keepdims=True)
        exponent = jnp.exp(scores - peak).astype(jnp.bfloat16)
        out = matmul(exponent, values[head])
        contexts.append(out / pltpu.roll(out, HD, 1))
        extended_ref[head] = extend(scaled, lane, head, 1.0, peak + jnp.log(out))
    context_ref[...] = jnp.where(lane < HD, contexts[0], contexts[1]).astype(jnp.bfloat16)


def attend_forward(length, qkv):
    seq_len = qkv.shape[0]
    pairs = qkv.shape[1] // (3 * PAIR)
    rows = min(256, seq_len)
    return pl.pallas_call(
        forward_kernel,
        grid_spec=pltpu.PrefetchScalarGridSpec(
            num_scalar_prefetch=1,
            grid=(pairs, seq_len // rows),
            in_specs=[
                pl.BlockSpec((rows, PAIR), lambda p, i, n: (i, 3 * p)),
                pl.BlockSpec((seq_len, PAIR), lambda p, i, n: (0, 3 * p + 1)),
                pl.BlockSpec((seq_len, PAIR), lambda p, i, n: (0, 3 * p + 2)),
            ],
            out_specs=[
                pl.BlockSpec((rows, PAIR), lambda p, i, n: (i, p)),
                pl.BlockSpec((2, rows, PAIR), lambda p, i, n: (p, i, 0)),
            ],
            scratch_shapes=[pltpu.VMEM((2, seq_len, PAIR), jnp.bfloat16)] * 2,
        ),
        out_shape=[
            jax.ShapeDtypeStruct((seq_len, pairs * PAIR), jnp.bfloat16),
            jax.ShapeDtypeStruct((2 * pairs, seq_len, PAIR), jnp.bfloat16),
        ],
        compiler_params=pltpu.CompilerParams(vmem_limit_bytes=VMEM_BYTES),
        cost_estimate=pl.CostEstimate(
            flops=8 * seq_len * seq_len * 2 * PAIR * pairs,
            bytes_accessed=12 * seq_len * PAIR * pairs,
            transcendentals=2 * seq_len * seq_len * pairs,
        ),
        name="attend_forward",
    )(length, qkv, qkv, qkv)


def backward_kernel(length_ref, extended_ref, k_ref, v_ref, context_ref, grad_ref, out_ref, grads, turned):
    step = pl.program_id(0)
    seq_len, rows = grad_ref.shape[0], k_ref.shape[0]

    @pl.when(step == 0)
    def _():
        def prepare(j, carry):
            here = pl.ds(pl.multiple_of(j * rows, rows), rows)
            lane = lanes(rows)
            grad = grad_ref[here, :].astype(jnp.float32)
            product = grad * context_ref[here, :].astype(jnp.float32)
            for head in range(2):
                centre = jnp.sum(
                    jnp.where(in_head(lane, head), product, 0.0), axis=1, keepdims=True
                )
                grads[head, here, :] = extend(grad, lane, head, 0.0, centre)
            return carry

        lax.fori_loop(0, seq_len // rows, prepare, 0)

    lane = lanes(rows)
    k_float = k_ref[...].astype(jnp.float32)
    v_float = v_ref[...].astype(jnp.float32)
    across = k_float.T.astype(jnp.bfloat16)
    key_grads, value_grads = [], []
    for head in range(2):
        keys = extend_keys(k_float, lane, head, step * rows, length_ref[0])
        values = extend_values(v_float, lane, head)
        query, grad = extended_ref[head], grads[head]
        probs = jnp.exp(times_rows(keys, query))
        score_grad = (probs * times_rows(values, grad)).astype(jnp.bfloat16)
        value_grads.append(matmul(probs.astype(jnp.bfloat16), grad))
        key_grads.append(matmul(score_grad, query))
        own = slice(HD * head, HD * (head + 1))
        part = matmul(across[own], score_grad)

        @pl.when(step == 0)
        def _():
            turned[own, :] = part

        @pl.when(step > 0)
        def _():
            turned[own, :] += part

    here = pl.ds(pl.multiple_of(step * rows, rows), rows)
    key_grad = jnp.where(lane < HD, key_grads[0], key_grads[1])
    value_grad = jnp.where(lane < HD, value_grads[0], value_grads[1])
    out_ref[here, PAIR : 2 * PAIR] = key_grad.astype(jnp.bfloat16)
    out_ref[here, 2 * PAIR :] = value_grad.astype(jnp.bfloat16)

    @pl.when(step == pl.num_programs(0) - 1)
    def _():
        def finish(j, carry):
            here = pl.ds(pl.multiple_of(j * rows, rows), rows)
            out_ref[here, :PAIR] = (turned[:, here].T * HD**-0.5).astype(jnp.bfloat16)
            return carry

        lax.fori_loop(0, seq_len // rows, finish, 0)


def attend_backward(length, extended, qkv, context, context_grad, pair):
    seq_len = qkv.shape[0]
    rows = min(256, seq_len)
    return pl.pallas_call(
        backward_kernel,
        grid_spec=pltpu.PrefetchScalarGridSpec(
            num_scalar_prefetch=1,
            grid=(seq_len // rows,),
            in_specs=[
                pl.BlockSpec((2, seq_len, PAIR), lambda i, n: (pair, 0, 0)),
                pl.BlockSpec((rows, PAIR), lambda i, n: (i, 3 * pair + 1)),
                pl.BlockSpec((rows, PAIR), lambda i, n: (i, 3 * pair + 2)),
                pl.BlockSpec((seq_len, PAIR), lambda i, n: (0, pair)),
                pl.BlockSpec((seq_len, PAIR), lambda i, n: (0, pair)),
            ],
            out_specs=pl.BlockSpec((seq_len, 3 * PAIR), lambda i, n: (0, 0)),
            scratch_shapes=[
                pltpu.VMEM((2, seq_len, PAIR), jnp.bfloat16),
                pltpu.VMEM((PAIR, seq_len), jnp.float32),
            ],
        ),
        out_shape=jax.ShapeDtypeStruct((seq_len, 3 * PAIR), jnp.bfloat16),
        compiler_params=pltpu.CompilerParams(vmem_limit_bytes=VMEM_BYTES),
        cost_estimate=pl.CostEstimate(
            flops=20 * seq_len * seq_len * 2 * PAIR,
            bytes_accessed=20 * seq_len * PAIR,
            transcendentals=2 * seq_len * seq_len,
        ),
        name="attend_backward",
    )(length, extended, qkv, qkv, context, context_grad)


def tie(*values):
    return lax.optimization_barrier(values)


def flip(array_in, axis_name, bits):
    size = lax.axis_size(axis_name)
    return lax.ppermute(array_in, axis_name, [(i, i ^ bits) for i in range(size)])


def total(array_in, axis_names):
    for name in axis_names:
        bits = 1
        while bits < lax.axis_size(name):
            array_in = array_in + flip(array_in, name, bits)
            bits *= 2
    return array_in


def shards(
    hidden_in,
    lengths,
    query_weight,
    query_bias,
    key_weight,
    value_weight,
    value_bias,
    output_weight,
    output_bias,
    first_gain,
    first_shift,
    inner_weight,
    inner_bias,
    outer_weight,
    outer_bias,
    second_gain,
    second_shift,
    cotangent,
    teacher,
):
    seq_len, model_width = hidden_in.shape
    ranks = lax.axis_size("tensor")
    rank = lax.axis_index("tensor")
    copies = lax.axis_size("dp")
    copy = lax.axis_index("dp")
    share_rows = seq_len // ranks
    heads_width = query_weight.shape[1]
    units = inner_weight.shape[1]
    pairs = heads_width // PAIR
    row_valid = jnp.arange(seq_len, dtype=jnp.int32) < lengths[0]

    def take_own(array_in):
        return lax.dynamic_slice_in_dim(array_in, rank * share_rows, share_rows, 0)

    def by_pairs(*arrays):
        return jnp.concatenate(
            [a[..., p * PAIR : (p + 1) * PAIR] for p in range(pairs) for a in arrays], axis=-1
        )

    def own_part(weight):
        rows = weight.shape[0] // copies
        return lax.dynamic_slice_in_dim(weight, copy * rows, rows, 0)

    def others(part):
        return jnp.stack([flip(part, "tensor", s) for s in range(1, ranks)])

    def gathered(parts):
        return lax.all_gather(parts, "dp", axis=1, tiled=True)

    def trade(blocks):
        return lax.all_to_all(blocks, "tensor", 0, 0)

    def block_of(blocks, s):
        return lax.dynamic_index_in_dim(blocks, rank ^ s, 0, keepdims=False)

    def reordered(blocks):
        return jnp.stack([block_of(blocks, s) for s in range(ranks)])

    def column_blocks(array_in):
        width = array_in.shape[1] // ranks
        return jnp.stack(
            [
                lax.dynamic_slice_in_dim(array_in, (rank ^ i) * width, width, 1)
                for i in range(ranks)
            ]
        )

    def add_blocks(blocks):
        return sum(blocks[i].astype(jnp.float32) for i in range(ranks))

    def ordered(vector_in):
        table = vector_in.reshape(ranks, -1)
        return jnp.concatenate(
            [lax.dynamic_index_in_dim(table, rank ^ s, 0, keepdims=False) for s in range(ranks)]
        )

    def half_columns(array_in, other):
        blocks = jnp.split(array_in, copies, axis=1)
        odd = ((copy & 1) ^ other) == 1
        return jnp.concatenate(
            [jnp.where(odd, blocks[i + 1], blocks[i]) for i in range(0, copies, 2)], axis=1
        )

    def half_rows(whole, other):
        blocks = whole.reshape(copies // 2, 2, -1, whole.shape[1])
        mine = lax.dynamic_index_in_dim(blocks, (copy & 1) ^ other, 1, keepdims=False)
        return mine.reshape(-1, whole.shape[1])

    def with_other_core(kept, given):
        come = flip(given, "dp", 1).astype(jnp.float32)
        return (kept.astype(jnp.float32) + come).astype(jnp.bfloat16)

    def qkv_product(qkv_low):
        return [matmul(half, qkv_low).astype(jnp.bfloat16) for half in hidden_halves]

    def to_chips(kept):
        blocks = [part.reshape(copies // 2, -1, part.shape[1]) for part in kept]
        rows = []
        for t in range(copies // 2):
            pieces = [
                lax.dynamic_index_in_dim(b, (copy >> 1) ^ t, 0, keepdims=False) for b in blocks
            ]
            rows.append(jnp.concatenate(pieces, axis=1))
        return [rows[0]] + [flip(rows[t], "dp", 2 * t) for t in range(1, copies // 2)]

    def add_all(parts):
        return sum(part.astype(jnp.float32) for part in parts)

    def scatter_copies(whole):
        return lax.psum_scatter(whole, "dp", scatter_dimension=0, tiled=True)

    def column_sums(array_in):
        return jnp.sum(array_in.astype(jnp.float32), axis=0)

    qkv_weight = by_pairs(query_weight, key_weight, value_weight)
    qkv_bias = by_pairs(query_bias, jnp.zeros_like(query_bias), value_bias)
    output_part, both_part = own_part(output_weight), own_part(
        jnp.concatenate([inner_weight, outer_weight], axis=1)
    )
    part_rows = output_part.shape[0]
    bias_rows = inner_bias.reshape(-1, heads_width)
    output_part = jnp.concatenate([output_part, bias_rows, jnp.zeros_like(bias_rows)])
    output_parts = trade(jnp.broadcast_to(output_part, (ranks, *output_part.shape)))
    near_part = flip(both_part, "tensor", 1)
    qkv_part = own_part(qkv_weight)
    qkv = (matmul(hidden_in, qkv_weight) + qkv_bias).astype(jnp.bfloat16)
    output_parts, near_part, qkv = tie(output_parts, near_part, qkv)
    far_parts = [flip(both_part, "tensor", s) for s in range(2, ranks)]
    output_others = [block_of(output_parts, s) for s in range(1, ranks)]
    output_rest = [p[:part_rows] for p in output_others]
    biases = [p[part_rows : part_rows + bias_rows.shape[0]] for p in output_others]

    column = lax.broadcasted_iota(jnp.int32, (part_rows, PAIR), 1)
    digits = jnp.where(column == 0, lengths[0] // 256, lengths[0] % 256).astype(jnp.bfloat16)
    near_rows = lax.all_gather(
        jnp.concatenate([near_part, *output_rest, digits], axis=1), "dp", axis=0, tiled=True
    )
    context, extended = attend_forward(lengths, qkv)
    received = trade(context.reshape(ranks, share_rows, heads_width))
    far_parts, context, hidden_late = tie(far_parts, context, hidden_in)
    far_rows = gathered(jnp.stack([p[:, i : i + units] for p in far_parts for i in (0, units)]))
    hidden_halves = [half_columns(hidden_late, other).T for other in range(2)]
    received, hidden_halves = tie(received, hidden_halves)
    digits = near_rows[::part_rows, -PAIR:].astype(jnp.float32)
    token_total = jnp.sum(256.0 * digits[:, 0] + digits[:, 1])
    grad_scale = seq_len * copies / (2.0 * token_total)
    context_all = jnp.concatenate(
        [block_of(received, s) for s in range(ranks)], axis=1
    )
    inner_weights = [inner_weight, near_rows[:, :units]]
    outer_weights = [outer_weight, near_rows[:, units : 2 * units]]
    for i in range(ranks - 2):
        inner_weights.append(far_rows[2 * i])
        outer_weights.append(far_rows[2 * i + 1])
    inner_biases = [inner_bias] + [b.reshape(-1) for b in biases]
    output_weight_all = jnp.concatenate([output_weight, near_rows[:, 2 * units : -PAIR]], axis=1)

    hidden_own = take_own(hidden_in).astype(jnp.float32)
    attention = times_rows(context_all, output_weight_all)
    normed, normal_one, inverse_one = layer_norm(
        hidden_own + (attention + output_bias), first_gain, first_shift
    )
    normed_low = normed.astype(jnp.bfloat16)
    activated, slopes = [], []
    branch = outer_bias.astype(jnp.float32)
    for s in range(ranks):
        value, slope = gelu_parts(matmul(normed_low, inner_weights[s]) + inner_biases[s])
        activated.append(value.astype(jnp.bfloat16))
        slopes.append(slope.astype(jnp.bfloat16))
        branch = branch + times_rows(activated[s], outer_weights[s])
    final, normal_two, inverse_two = layer_norm(normed + branch, second_gain, second_shift)
    row_mask = take_own(row_valid)[:, None]
    difference = final - take_own(teacher).astype(jnp.float32)
    loss_part = jnp.sum(jnp.where(row_mask, difference * difference, 0.0))
    final_grad = jnp.where(
        row_mask, take_own(cotangent).astype(jnp.float32) + grad_scale * difference, 0.0
    )
    second_grad = norm_back(final_grad, normal_two, inverse_two, second_gain)
    branch_low = second_grad.astype(jnp.bfloat16)
    outer_whole = over_rows(branch_low, jnp.concatenate(activated, axis=1)).astype(jnp.bfloat16)
    outer_whole, branch_low, qkv_part = tie(outer_whole, branch_low, qkv_part)
    outer_rows = scatter_copies(outer_whole)
    qkv_parts = others(qkv_part)
    inner_lows = []
    normed_grad = second_grad
    for s in range(ranks):
        inner_low = (matmul(branch_low, outer_weights[s]) * slopes[s]).astype(jnp.bfloat16)
        inner_lows.append(inner_low)
        normed_grad = normed_grad + times_rows(inner_low, inner_weights[s])
    first_grad = norm_back(normed_grad, normal_one, inverse_one, first_gain)
    attention_low = first_grad.astype(jnp.bfloat16)
    grad_all = matmul(attention_low, output_weight_all).astype(jnp.bfloat16)
    grad_all, inner_lows, qkv_parts, attention_late = tie(
        grad_all, inner_lows, qkv_parts, attention_low
    )
    context_grad = trade(column_blocks(grad_all)).reshape(seq_len, heads_width)
    inner_whole = over_rows(normed_low, jnp.concatenate(inner_lows, axis=1)).astype(jnp.bfloat16)
    inner_kept = [
        with_other_core(half_rows(half, 0), half_rows(half, 1))
        for half in jnp.split(inner_whole, 2, axis=1)
    ]
    output_whole = over_rows(attention_late, context_all).astype(jnp.bfloat16)
    inner_chips = to_chips(inner_kept)
    vectors = [
        ordered(jnp.concatenate([column_sums(low) for low in inner_lows])),
        column_sums(attention_low),
        column_sums(normed_grad * normal_one),
        column_sums(normed_grad),
        column_sums(branch_low),
        column_sums(final_grad * normal_two),
        column_sums(final_grad),
        ordered(column_sums(grad_all)),
        jnp.full((model_width,), loss_part),
    ]
    vectors = jnp.concatenate([v.reshape(-1, model_width) for v in vectors])
    vectors = vectors + flip(vectors, "dp", 1)
    outer_blocks = column_blocks(outer_rows)
    context_grad, vectors, output_whole, outer_blocks = tie(
        context_grad, vectors, output_whole, outer_blocks
    )
    outer_come = trade(outer_blocks)
    rank_bits = [1 << p for p in range(ranks.bit_length() - 1)]
    vector_come = flip(vectors, "tensor", rank_bits[0])

    def add_input(rows, moved, pair):
        columns = slice(3 * PAIR * pair, 3 * PAIR * (pair + 1))
        blocks = jnp.concatenate([block_of(moved, s) for s in range(ranks)], axis=1)
        weights = [qkv_weight] + [qkv_rest[s] for s in range(ranks - 1)]
        return rows + times_rows(blocks, jnp.concatenate([w[:, columns] for w in weights], axis=1))

    input_rows = first_grad
    query_sums = []
    for pair in range(pairs):
        qkv_low = attend_backward(lengths, extended, qkv, context, context_grad, pair)
        if pair == 0:
            qkv_low, inner_chips, outer_come, vector_come, qkv_parts, output_whole = tie(
                qkv_low, inner_chips, outer_come, vector_come, qkv_parts, output_whole
            )
            output_rows = scatter_copies(output_whole)
            qkv_rest = gathered(qkv_parts)
            inner_rows = add_all(inner_chips).astype(jnp.bfloat16)
            inner_parts = jnp.split(inner_rows, ranks, axis=1)
            vectors = vectors + vector_come
            vector_come = flip(vectors, "tensor", rank_bits[1])
        if pair == 0:
            qkv_kept = [with_other_core(*qkv_product(qkv_low))]
            context_grad, qkv_kept, inner_parts = tie(context_grad, qkv_kept, inner_parts)
            inner_come = [flip(inner_parts[t], "tensor", t) for t in range(1, ranks)]
        else:
            moved, qkv_low, inner_come, vector_come, output_rows, qkv_kept = tie(
                moved, qkv_low, inner_come, vector_come, output_rows, qkv_kept
            )
            vectors = vectors + vector_come
            input_rows = add_input(input_rows, moved, pair - 1)
            qkv_kept.append(with_other_core(*qkv_product(qkv_low)))
        moved = trade(qkv_low.reshape(ranks, share_rows, -1))
        query_sums.append(column_sums(qkv_low[:, :PAIR]))
    if pairs == 1:
        vectors = vectors + vector_come
    for bit in rank_bits[2:]:
        vectors = vectors + flip(vectors, "tensor", bit)
    query_sums = jnp.concatenate(query_sums)
    query_sums = query_sums + flip(query_sums, "dp", 1)
    query_row = jnp.pad(query_sums, (0, model_width - heads_width))[None]
    vectors = jnp.concatenate([vectors, query_row])
    for place in range(1, copies.bit_length() - 1):
        vectors = vectors + flip(vectors, "dp", 1 << place)
    query_sums = vectors[-1, :heads_width]

    high = query_sums.astype(jnp.bfloat16)
    middle = (query_sums - high.astype(jnp.float32)).astype(jnp.bfloat16)
    low = query_sums - high.astype(jnp.float32) - middle.astype(jnp.float32)
    digit_rows = jnp.stack([high, middle, low.astype(jnp.bfloat16)])
    digit_rows = jnp.pad(digit_rows, ((0, 5), (0, 0)))
    last = [jnp.concatenate([part, digit_rows]) for part in jnp.split(output_rows, ranks, axis=1)]
    last = reordered(jnp.stack(last))
    moved, last, outer_come, inner_come = tie(moved, last, outer_come, inner_come)
    outer_weight_grad = add_blocks(outer_come)
    inner_weight_grad = add_all([inner_parts[0], *inner_come])
    qkv_sums = add_all(to_chips(qkv_kept))
    input_rows = add_input(input_rows, moved, pairs - 1)
    last = trade(last)
    output_weight_grad = add_blocks(last[:, :part_rows])
    digit_rows = last[:, part_rows:].astype(jnp.float32)
    query_bias_grad = (digit_rows[:, 0] + digit_rows[:, 1] + digit_rows[:, 2]).reshape(-1)
    qkv_sums = jnp.split(qkv_sums, 3 * pairs, axis=1)
    query_weight_grad, key_weight_grad, value_weight_grad = [
        jnp.concatenate(qkv_sums[i::3], axis=1) for i in range(3)
    ]

    wide = ranks * units // model_width
    inner_bias_grad = vectors[:wide].reshape(-1)
    (
        output_bias_grad,
        first_gain_grad,
        first_shift_grad,
        outer_bias_grad,
        second_gain_grad,
        second_shift_grad,
        value_bias_grad,
    ) = [vectors[wide + i] for i in range(7)]
    return (
        final.astype(jnp.bfloat16),
        vectors[wide + 7, 0] / token_total,
        input_rows,
        query_weight_grad,
        query_bias_grad,
        key_weight_grad,
        value_weight_grad,
        value_bias_grad,
        output_weight_grad,
        output_bias_grad,
        first_gain_grad,
        first_shift_grad,
        inner_weight_grad,
        inner_bias_grad,
        outer_weight_grad,
        outer_bias_grad,
        second_gain_grad,
        second_shift_grad,
    )


def solution(mesh):
    rows, columns, split = P("dp", None), P(None, "tensor"), P("dp", "tensor")
    part, whole, own = P("tensor"), P(), P(("dp", "tensor"), None)
    in_specs = (
        rows,
        P("dp"),
        columns,
        part,
        columns,
        columns,
        part,
        columns,
        whole,
        whole,
        whole,
        columns,
        part,
        columns,
        whole,
        whole,
        whole,
        rows,
        rows,
    )
    out_specs = (
        own,
        whole,
        own,
        split,
        whole,
        split,
        split,
        whole,
        split,
        whole,
        whole,
        whole,
        split,
        whole,
        split,
        whole,
        whole,
        whole,
    )
    return jax.shard_map(shards, mesh=mesh, in_specs=in_specs, out_specs=out_specs, check_vma=False)
```
